32 devices in a mesh: groups: 2 (over x), seq: 16 (over z, y, core).
Axes of the slice: x: 2, y: 2, z: 4, core: 2. Of those that a mesh axis runs over, the one named last changes fastest.
Arguments:
- queries: bfloat16 [8192, 768], P(('groups', 'seq')), parts along dimension 0, may hold values from -6 to 6
- keys_values: bfloat16 [2, 8192, 768], P(None, ('groups', 'seq')), parts along dimension 1, may hold values from -6 to 6
- cotangent: bfloat16 [8192, 768], P(('groups', 'seq')), parts along dimension 0, may hold values from -6 to 6
- frame_lists: int32 [64, 6], P(('groups', 'seq')), parts along dimension 0, may hold values from 0 to 15
- sink_owner: int32 [2], P('groups'), parts along dimension 0, may hold values from 0 to 15
Outputs:
- attended: bfloat16 [8192, 768], P(('groups', 'seq')), parts along dimension 0
- grad_queries: bfloat16 [8192, 768], P(('groups', 'seq')), parts along dimension 0
- grad_keys_values: bfloat16 [2, 8192, 768], P(None, ('groups', 'seq')), parts along dimension 1
The draws below stay inside these ranges and needn't reach their ends.
There are 2 independent parts, one for each index of `groups`. The reference program is written for one: setup_inputs(seed, part) draws one part's arguments, and reference() takes and returns one part's arrays. A program takes and returns all parts, laid end to end along the dimension named above; each array names one. Nothing has to cross between parts.
Inputs may be any that keep to these rules, and one draw needn't show every extreme that they name: `frame_lists`: entries may repeat within a row.
All inputs are finite; a program needn't handle non-finite values.
Results may differ from the reference program's by a relative error of at most 0.025.
Values may be sent and summed in bfloat16 or wider, within the bound.
A program may use at most 128 MiB of HBM per device.

```python
import math
from functools import partial
import jax
import jax.numpy as jnp
from jax import lax

HEADS = 12
HEAD = 64
BLK = 128
SSEL = 6
CB = 1
TOKENS = 4096
NQB = 32
N_SEQ = 16


def drawn_part(key, salt):
    return jnp.clip(jax.random.normal(jax.random.fold_in(key, salt), (TOKENS, HEADS * HEAD)), -6.0, 6.0)


def draw_queries(key, part):
    values = drawn_part(key, 1)
    return values.astype(jnp.bfloat16)


def draw_keys_values(key, part):
    key_part = drawn_part(key, 11)
    value_part = drawn_part(key, 21)
    return jnp.stack((key_part, value_part)).astype(jnp.bfloat16)


def touch_ends(values, own_key, smallest, top_value):
    dims = values.shape
    place = [jax.random.randint(jax.random.fold_in(own_key, axis), (), 0, dims[axis]) for axis in range(len(dims))]
    values = values.at[tuple(place)].set(smallest)
    longest = dims.index(max(dims))
    place[longest] = (place[longest] + 1) % dims[longest]
    return values.at[tuple(place)].set(top_value)


def level_of(stream_key, dims, shards, least, largest):
    gain, own = 1.0, jax.random.fold_in(stream_key, 6)
    for dim, blocks in shards:
        draws = jnp.exp(jax.random.uniform(jax.random.fold_in(own, dim), (blocks,), jnp.float32, least / len(shards), largest / len(shards)))
        gain = gain * jnp.repeat(draws, dims[dim] // blocks).reshape([-1 if axis == dim else 1 for axis in range(len(dims))])
    return gain


def bell_draw(stream_key, extent, scale, bound, shards=(), kind=jnp.bfloat16):
    factor_of = level_of(stream_key, extent, shards, -0.22, 0.18) if shards else 1.0
    result = jax.random.normal(stream_key, extent, jnp.float32) * scale * factor_of
    return jnp.minimum(jnp.maximum(result, -bound), bound).astype(kind)


def setup_inputs(seed: int = 0, part: int = 0) -> dict:
    key_of = jax.random.split(jax.random.key(seed), 6)
    part_splits = jax.random.split(jax.random.fold_in(key_of[5], part), 6)
    queries = draw_queries(jax.random.fold_in(jax.random.fold_in(key_of[5], part), 71), part)
    keys_values = draw_keys_values(jax.random.fold_in(jax.random.fold_in(key_of[5], part), 71), part)
    cotangent = bell_draw(part_splits[2], (TOKENS, HEADS * HEAD), 1.0, 6.0, ((0, 16),))
    frame_lists = touch_ends(jax.random.randint(part_splits[3], (NQB, SSEL), 0, N_SEQ), jax.random.fold_in(part_splits[3], 1), 0, N_SEQ - 1).astype(jnp.int32)
    sink_owner = jax.random.randint(part_splits[4], (1,), 0, N_SEQ).astype(jnp.int32)
    return {"queries": queries, "keys_values": keys_values, "cotangent": cotangent, "frame_lists": frame_lists, "sink_owner": sink_owner}


def anchor_span(device_ids, axis_length):
    return jnp.where(device_ids % 2 == 0, device_ids, 2 * axis_length - 1 - device_ids)

def build_masks(frame_ids, span_index, sink_device, axis_length, row_count):
    block_count, entry_count = frame_ids.shape
    entry_order = jnp.arange(entry_count)
    repeated = jnp.any((frame_ids[:, :, None] == frame_ids[:, None, :]) & (entry_order[None, None, :] < entry_order[None, :, None]), axis=2)
    is_valid = (anchor_span(frame_ids, axis_length) < span_index) & (frame_ids != sink_device) & jnp.logical_not(repeated)
    key_valid = jnp.repeat(jnp.repeat(is_valid, BLK, axis=1), row_count // block_count, axis=0)
    position = jnp.arange(row_count)
    in_sink = (span_index == anchor_span(sink_device, axis_length)) & (position < BLK)
    window = (position[None, :] <= position[:, None]) & jnp.logical_not(in_sink[None, :])
    return (window, key_valid)

def widen(matrix):
    return matrix.astype(jnp.float32)

def tier_products(left_rows, right_rows, picked_right, sink_right):
    row_count = left_rows.shape[0]
    block_count = picked_right.shape[0]
    left_heads = widen(left_rows).reshape(row_count, -1, HEAD)
    window_part = jnp.einsum('qhd,khd->hqk', left_heads, widen(right_rows).reshape(row_count, -1, HEAD))
    sink_part = jnp.einsum('qhd,khd->hqk', left_heads, widen(sink_right).reshape(BLK, -1, HEAD))
    left_blocks = widen(left_rows).reshape(block_count, row_count // block_count, -1, HEAD)
    right_blocks = widen(picked_right).reshape(block_count, picked_right.shape[1], -1, HEAD)
    anchor_part = jnp.einsum('bqhd,bkhd->hbqk', left_blocks, right_blocks)
    return (window_part, sink_part, anchor_part.reshape(left_heads.shape[1], row_count, -1))

def tier_scores(query_rows, key_rows, picked_keys, sink_keys, window, key_valid):
    score_scale = 1.0 / math.sqrt(HEAD)
    window_part, sink_part, anchor_part = tier_products(query_rows, key_rows, picked_keys, sink_keys)
    window_part = jnp.where(window[None], window_part * score_scale, -jnp.inf)
    anchor_part = jnp.where(key_valid[None], anchor_part * score_scale, -jnp.inf)
    return (window_part, sink_part * score_scale, anchor_part)

def normalized(scores):
    window_part, sink_part, anchor_part = scores
    row_max = jnp.maximum(jnp.maximum(lax.optimization_barrier(jnp.max(window_part, axis=-1)), lax.optimization_barrier(jnp.max(sink_part, axis=-1))), lax.optimization_barrier(jnp.max(anchor_part, axis=-1)))
    summed = lax.optimization_barrier(jnp.sum(jnp.exp(window_part - row_max[..., None]), axis=-1))
    summed = summed + lax.optimization_barrier(jnp.sum(jnp.exp(sink_part - row_max[..., None]), axis=-1))
    summed = summed + lax.optimization_barrier(jnp.sum(jnp.exp(anchor_part - row_max[..., None]), axis=-1))
    log_total = row_max + jnp.log(summed)
    return (jnp.exp(window_part - log_total[..., None]), jnp.exp(sink_part - log_total[..., None]), jnp.exp(anchor_part - log_total[..., None]))

def rounded(matrix):
    return lax.optimization_barrier(matrix.astype(jnp.bfloat16)).astype(jnp.float32)

def lowered(weights):
    return (rounded(weights[0]), rounded(weights[1]), rounded(weights[2]))

def attend(weights, window_rows, picked_rows, sink_rows):
    head_count, row_count = (weights[0].shape[0], weights[0].shape[1])
    block_count = picked_rows.shape[0]
    summed = jnp.einsum('hqk,khd->qhd', weights[0], widen(window_rows).reshape(row_count, -1, HEAD))
    summed = summed + jnp.einsum('hqk,khd->qhd', weights[1], widen(sink_rows).reshape(BLK, -1, HEAD))
    anchor_weights = weights[2].reshape(head_count, block_count, row_count // block_count, -1)
    anchor_part = jnp.einsum('hbqk,bkhd->bqhd', anchor_weights, widen(picked_rows).reshape(block_count, picked_rows.shape[1], -1, HEAD))
    return (summed + anchor_part.reshape(row_count, head_count, HEAD)).reshape(row_count, -1)

def key_side(weights, left_rows, block_count):
    head_count, row_count = (weights[0].shape[0], weights[0].shape[1])
    model_width = left_rows.shape[1]
    left_heads = widen(left_rows).reshape(row_count, -1, HEAD)
    window_part = jnp.einsum('hqk,qhd->khd', weights[0], left_heads).reshape(row_count, model_width)
    sink_part = jnp.einsum('hqk,qhd->khd', weights[1], left_heads).reshape(BLK, model_width)
    anchor_weights = weights[2].reshape(head_count, block_count, row_count // block_count, -1)
    left_blocks = widen(left_rows).reshape(block_count, row_count // block_count, -1, HEAD)
    anchor_part = jnp.einsum('hbqk,bqhd->bkhd', anchor_weights, left_blocks).reshape(-1, BLK, model_width)
    return (window_part, sink_part, anchor_part)

def forward_span(query_rows, key_rows, value_rows, picked_keys, picked_values, window, key_valid, sink_keys, sink_values):
    weights = normalized(tier_scores(query_rows, key_rows, picked_keys, sink_keys, window, key_valid))
    return attend(lowered(weights), value_rows, picked_values, sink_values).astype(jnp.bfloat16)

def backward_span(query_rows, key_rows, value_rows, grad_rows, attended_rows, picked_keys, picked_values, window, key_valid, sink_keys, sink_values):
    row_count = query_rows.shape[0]
    block_count = picked_keys.shape[0]
    score_scale = 1.0 / math.sqrt(HEAD)
    weights = normalized(tier_scores(query_rows, key_rows, picked_keys, sink_keys, window, key_valid))
    weights_low = lowered(weights)
    row_delta = lax.optimization_barrier(jnp.sum(widen(grad_rows).reshape(row_count, -1, HEAD) * widen(attended_rows).reshape(row_count, -1, HEAD), axis=-1)).T[..., None]
    products = tier_products(grad_rows, value_rows, picked_values, sink_values)
    dscores = (rounded(weights[0] * (products[0] - row_delta) * score_scale), rounded(weights[1] * (products[1] - row_delta) * score_scale), rounded(weights[2] * (products[2] - row_delta) * score_scale))
    grad_query = attend(dscores, key_rows, picked_keys, sink_keys)
    key_grads = key_side(dscores, query_rows, block_count)
    value_grads = key_side(weights_low, grad_rows, block_count)
    local_grads = jnp.stack((key_grads[0], value_grads[0]))
    entries = jnp.stack((jnp.concatenate((key_grads[2], key_grads[1][None]), axis=0), jnp.concatenate((value_grads[2], value_grads[1][None]), axis=0)), axis=1)
    return (grad_query, local_grads, entries)

def reference(queries, keys_values, cotangent, frame_lists, sink_owner):
    half_rows = CB * BLK
    row_count = 2 * half_rows
    model_width = HEADS * HEAD
    sink_device = sink_owner[0].astype(jnp.int32)
    device_ids = jnp.arange(N_SEQ, dtype=jnp.int32)
    anchor_starts = (device_ids * row_count + jnp.where(device_ids % 2 == 0, 0, half_rows)).astype(jnp.int32)
    anchors = jax.vmap(lambda first_row: lax.dynamic_slice_in_dim(keys_values, first_row, BLK, axis=1), out_axes=1)(anchor_starts)
    sink_pair = anchors[:, sink_device]
    masker = jax.vmap(partial(build_masks, axis_length=N_SEQ, row_count=half_rows), in_axes=(0, 0, None))
    forward = jax.vmap(forward_span, in_axes=(0, 0, 0, 0, 0, 0, 0, None, None))
    backward = jax.vmap(backward_span, in_axes=(0, 0, 0, 0, 0, 0, 0, 0, 0, None, None))

    def device_step(running, device_index):
        first_row = (device_index * row_count).astype(jnp.int32)
        query_slots = lax.dynamic_slice_in_dim(queries, first_row, row_count, 0).reshape(2, half_rows, model_width)
        pair_rows = lax.dynamic_slice_in_dim(keys_values, first_row, row_count, 1).reshape(2, 2, half_rows, model_width)
        grad_slots = lax.dynamic_slice_in_dim(cotangent, first_row, row_count, 0).reshape(2, half_rows, model_width)
        frame_slots = lax.dynamic_slice_in_dim(frame_lists, (device_index * 2 * CB).astype(jnp.int32), 2 * CB, 0).reshape(2, CB, SSEL)
        span_ids = jnp.stack((device_index, 2 * N_SEQ - 1 - device_index)).astype(jnp.int32)
        window, key_valid = masker(frame_slots, span_ids, sink_device)
        picked = anchors[:, frame_slots].reshape(2, 2, CB, SSEL * BLK, model_width)
        attended_slots = forward(query_slots, pair_rows[0], pair_rows[1], picked[0], picked[1], window, key_valid, sink_pair[0], sink_pair[1])
        grad_query, local_grads, entries = backward(query_slots, pair_rows[0], pair_rows[1], grad_slots, attended_slots, picked[0], picked[1], window, key_valid, sink_pair[0], sink_pair[1])
        owner_ids = jnp.concatenate((frame_slots.reshape(2, -1), jnp.broadcast_to(sink_device, (2, 1))), axis=1).reshape(-1)
        selector = (owner_ids[:, None] == device_ids[None, :]).astype(jnp.float32)
        device_sum = jnp.einsum('ej,ekbd->jkbd', selector, entries.reshape(-1, 2, BLK, model_width), precision=lax.Precision.HIGHEST)
        outputs = (attended_slots.reshape(row_count, model_width), grad_query.reshape(row_count, model_width).astype(jnp.bfloat16), local_grads.transpose(1, 0, 2, 3).reshape(2, row_count, model_width))
        return (running + rounded(device_sum), outputs)
    zero_sums = jnp.zeros((N_SEQ, 2, BLK, model_width), jnp.float32)
    totals, stacked = lax.scan(device_step, zero_sums, device_ids)
    attended, grad_queries, local_grads = stacked

    def place_rows(device_grads, anchor_sum, device_index):
        offset = jnp.where(device_index % 2 == 0, 0, half_rows).astype(jnp.int32)
        rows_now = lax.dynamic_slice_in_dim(device_grads, offset, BLK, 1) + anchor_sum
        return lax.dynamic_update_slice_in_dim(device_grads, rows_now, offset, 1)
    placed = jax.vmap(place_rows)(local_grads, totals, device_ids)
    grad_keys_values = placed.transpose(1, 0, 2, 3).reshape(2, N_SEQ * row_count, model_width).astype(jnp.bfloat16)
    return (attended.reshape(-1, model_width), grad_queries.reshape(-1, model_width), grad_keys_values)
```

```python
import functools
import math

import jax
import jax.numpy as jnp
from jax import lax
from jax.experimental import pallas as pl
from jax.experimental.pallas import tpu as pltpu
from jax.sharding import PartitionSpec as P

HEAD = 64
BLK = 128
PAIR = 2 * HEAD
NEG = -1e30
VMEM_BYTES = 60 * 1024 * 1024


def anchor_span(device_id, axis_length):
    return jnp.where(device_id % 2 == 0, device_id, 2 * axis_length - 1 - device_id)


def stack_heads(rows, low):
    zero = jnp.zeros_like(rows)
    return jnp.concatenate((jnp.where(low, rows, zero), jnp.where(low, zero, rows)), axis=0)


def unstack_heads(rows, low):
    return jnp.where(low, rows[:BLK], rows[BLK:])


def dot_last(left, right):
    return lax.dot_general(left, right, (((1,), (1,)), ((), ())), preferred_element_type=jnp.float32)


def dot_first(left, right):
    return lax.dot_general(left, right, (((0,), (0,)), ((), ())), preferred_element_type=jnp.float32)


def attention_kernel(
    axis_length,
    frames_ref,
    sink_ref,
    q_ref,
    kv_ref,
    g_ref,
    anchors_ref,
    out_ref,
    grad_q_ref,
    local_ref,
    parts_ref,
):
    me = lax.axis_index("seq")
    sink = sink_ref[0]
    entries = frames_ref.shape[1]
    pairs = q_ref.shape[1] // PAIR
    scale = 1.0 / math.sqrt(HEAD)
    low = lax.broadcasted_iota(jnp.int32, (BLK, PAIR), 1) < HEAD
    row = lax.broadcasted_iota(jnp.int32, (2 * BLK, BLK), 0) % BLK
    causal = lax.broadcasted_iota(jnp.int32, (2 * BLK, BLK), 1) <= row

    @pl.loop(0, axis_length)
    def _(j):
        parts_ref[j] = jnp.zeros(parts_ref.shape[1:], parts_ref.dtype)

    for block in range(2):
        span = me if block == 0 else 2 * axis_length - 1 - me
        rows = pl.ds(block * BLK, BLK)
        ids = [frames_ref[block, e] for e in range(entries)]
        biases = []
        for e in range(entries):
            valid = (anchor_span(ids[e], axis_length) < span) & (ids[e] != sink)
            for earlier in range(e):
                valid = valid & (ids[e] != ids[earlier])
            biases.append(jnp.where(valid, 0.0, NEG))
        biases.append(None)
        slots = ids + [sink]
        window_scalar = jnp.where(span == anchor_span(sink, axis_length), NEG, 0.0)
        window_bias = jnp.where(causal, window_scalar, NEG)

        @pl.loop(0, pairs)
        def _(pair):
            cols = pl.ds(pl.multiple_of(pair * PAIR, PAIR), PAIR)
            q2 = stack_heads(q_ref[rows, cols] * jnp.bfloat16(scale), low)
            grad = g_ref[rows, cols]
            g2 = stack_heads(grad, low)
            keys = jnp.concatenate(
                [kv_ref[0, rows, cols]] + [anchors_ref[j, 0, :, cols] for j in slots], axis=0
            )
            values = jnp.concatenate(
                [kv_ref[1, rows, cols]] + [anchors_ref[j, 1, :, cols] for j in slots], axis=0
            )
            tiles = 1 + len(slots)
            scores = dot_last(q2, keys)
            parts = [scores[:, t * BLK : (t + 1) * BLK] for t in range(tiles)]
            parts[0] = parts[0] + window_bias
            for t in range(1, tiles - 1):
                parts[t] = parts[t] + biases[t - 1]
            top = functools.reduce(jnp.maximum, parts)
            top = jnp.max(top, axis=1, keepdims=True)
            weights = [jnp.exp(part - top) for part in parts]
            total = jnp.sum(functools.reduce(jnp.add, weights), axis=1, keepdims=True)
            inverse = 1.0 / total
            weights = [w * inverse for w in weights]
            weights_low = jnp.concatenate([w.astype(jnp.bfloat16) for w in weights], axis=1)
            out2 = jnp.dot(weights_low, values, preferred_element_type=jnp.float32)
            attended = unstack_heads(out2, low).astype(jnp.bfloat16)
            out_ref[rows, cols] = attended
            product = grad.astype(jnp.float32) * attended.astype(jnp.float32)
            delta = jnp.sum(stack_heads(product, low), axis=1, keepdims=True)
            dprobs = dot_last(g2, values)
            dscores = jnp.concatenate(
                [
                    (weights[t] * (dprobs[:, t * BLK : (t + 1) * BLK] - delta)).astype(jnp.bfloat16)
                    for t in range(tiles)
                ],
                axis=1,
            )
            grad2 = jnp.dot(dscores, keys, preferred_element_type=jnp.float32)
            grad_q_ref[rows, cols] = (unstack_heads(grad2, low) * scale).astype(jnp.bfloat16)
            for which, product in ((0, dot_first(dscores, q2)), (1, dot_first(weights_low, g2))):
                local_ref[which, rows, cols] = product[:BLK]
                for t in range(1, tiles):
                    j = slots[t - 1]
                    held = parts_ref[j, which, :, cols].astype(jnp.float32)
                    parts_ref[j, which, :, cols] = (
                        held + product[t * BLK : (t + 1) * BLK]
                    ).astype(jnp.bfloat16)


def attention(axis_length, frames, sink, queries, keys_values, cotangent, anchors):
    vmem = pl.BlockSpec(memory_space=pltpu.VMEM)
    smem = pl.BlockSpec(memory_space=pltpu.SMEM)
    return pl.pallas_call(
        functools.partial(attention_kernel, axis_length),
        out_shape=(
            jax.ShapeDtypeStruct(queries.shape, jnp.bfloat16),
            jax.ShapeDtypeStruct(queries.shape, jnp.bfloat16),
            jax.ShapeDtypeStruct(keys_values.shape, jnp.float32),
            jax.ShapeDtypeStruct(anchors.shape, jnp.bfloat16),
        ),
        in_specs=[smem, smem, vmem, vmem, vmem, vmem],
        out_specs=[vmem] * 4,
        compiler_params=pltpu.CompilerParams(vmem_limit_bytes=VMEM_BYTES),
        name="attention",
    )(frames, sink, queries, keys_values, cotangent, anchors)


def shards(queries, keys_values, cotangent, frame_lists, sink_owner):
    axis_length = lax.axis_size("seq")
    me = lax.axis_index("seq")
    offset = jnp.where(me % 2 == 0, 0, BLK).astype(jnp.int32)
    own_anchor = lax.dynamic_slice_in_dim(keys_values, offset, BLK, axis=1)
    anchors = lax.all_gather(own_anchor, "seq", axis=0, tiled=False)
    attended, grad_queries, local, parts = attention(
        axis_length, frame_lists, sink_owner, queries, keys_values, cotangent, anchors
    )
    reduced = lax.psum_scatter(parts, "seq", scatter_dimension=0, tiled=True)[0]
    anchor_rows = lax.dynamic_slice_in_dim(local, offset, BLK, axis=1) + reduced.astype(jnp.float32)
    local = lax.dynamic_update_slice_in_dim(local, anchor_rows, offset, axis=1)
    return attended, grad_queries, local.astype(jnp.bfloat16)


def solution(mesh):
    rows = P(("groups", "seq"), None)
    pairs = P(None, ("groups", "seq"), None)
    return jax.shard_map(
        shards,
        mesh=mesh,
        in_specs=(rows, pairs, rows, rows, P("groups")),
        out_specs=(rows, rows, pairs),
        check_vma=False,
    )
```

```python
import functools
import math

import jax
import jax.numpy as jnp
from jax import lax
from jax.experimental import pallas as pl
from jax.experimental.pallas import tpu as pltpu
from jax.sharding import PartitionSpec as P

HEAD = 64
BLK = 128
PAIR = 2 * HEAD
NEG = -1e30
VMEM_BYTES = 60 * 1024 * 1024


def anchor_span(device_id, axis_length):
    return jnp.where(device_id % 2 == 0, device_id, 2 * axis_length - 1 - device_id)


def stack_heads(rows, low):
    zero = jnp.zeros_like(rows)
    return jnp.concatenate((jnp.where(low, rows, zero), jnp.where(low, zero, rows)), axis=0)


def unstack_heads(rows, low):
    return jnp.where(low, rows[:BLK], rows[BLK:])


def dot_last(left, right):
    return lax.dot_general(left, right, (((1,), (1,)), ((), ())), preferred_element_type=jnp.float32)


def dot_first(left, right):
    return lax.dot_general(left, right, (((0,), (0,)), ((), ())), preferred_element_type=jnp.float32)


def attention_kernel(
    axis_length,
    frames_ref,
    sink_ref,
    q_ref,
    kv_ref,
    g_ref,
    anchors_ref,
    out_ref,
    grad_q_ref,
    local_ref,
    parts_ref,
):
    me = lax.axis_index("seq")
    sink = sink_ref[0]
    entries = frames_ref.shape[1]
    pairs = q_ref.shape[1] // PAIR
    scale = 1.0 / math.sqrt(HEAD)
    low = lax.broadcasted_iota(jnp.int32, (BLK, PAIR), 1) < HEAD
    row = lax.broadcasted_iota(jnp.int32, (2 * BLK, BLK), 0) % BLK
    causal = lax.broadcasted_iota(jnp.int32, (2 * BLK, BLK), 1) <= row

    @pl.loop(0, axis_length)
    def _(j):
        parts_ref[j] = jnp.zeros(parts_ref.shape[1:], parts_ref.dtype)

    for block in range(2):
        span = me if block == 0 else 2 * axis_length - 1 - me
        rows = pl.ds(block * BLK, BLK)
        ids = [frames_ref[block, e] for e in range(entries)]
        biases = []
        for e in range(entries):
            valid = (anchor_span(ids[e], axis_length) < span) & (ids[e] != sink)
            for earlier in range(e):
                valid = valid & (ids[e] != ids[earlier])
            biases.append(jnp.where(valid, 0.0, NEG))
        biases.append(None)
        slots = ids + [sink]
        window_scalar = jnp.where(span == anchor_span(sink, axis_length), NEG, 0.0)
        window_bias = jnp.where(causal, window_scalar, NEG)

        @pl.loop(0, pairs)
        def _(pair):
            cols = pl.ds(pl.multiple_of(pair * PAIR, PAIR), PAIR)
            q2 = stack_heads(q_ref[rows, cols] * jnp.bfloat16(scale), low)
            grad = g_ref[rows, cols]
            g2 = stack_heads(grad, low)
            keys = jnp.concatenate(
                [kv_ref[0, rows, cols]] + [anchors_ref[j, 0, :, cols] for j in slots], axis=0
            )
            values = jnp.concatenate(
                [kv_ref[1, rows, cols]] + [anchors_ref[j, 1, :, cols] for j in slots], axis=0
            )
            tiles = 1 + len(slots)
            scores = dot_last(q2, keys)
            parts = [scores[:, t * BLK : (t + 1) * BLK] for t in range(tiles)]
            parts[0] = parts[0] + window_bias
            for t in range(1, tiles - 1):
                parts[t] = parts[t] + biases[t - 1]
            top = functools.reduce(jnp.maximum, parts)
            top = jnp.max(top, axis=1, keepdims=True)
            weights = [jnp.exp(part - top) for part in parts]
            total = jnp.sum(functools.reduce(jnp.add, weights), axis=1, keepdims=True)
            inverse = 1.0 / total
            weights = [w * inverse for w in weights]
            weights_low = jnp.concatenate([w.astype(jnp.bfloat16) for w in weights], axis=1)
            out2 = jnp.dot(weights_low, values, preferred_element_type=jnp.float32)
            attended = unstack_heads(out2, low).astype(jnp.bfloat16)
            out_ref[rows, cols] = attended
            product = grad.astype(jnp.float32) * attended.astype(jnp.float32)
            delta = jnp.sum(stack_heads(product, low), axis=1, keepdims=True)
            dprobs = dot_last(g2, values)
            dscores = jnp.concatenate(
                [
                    (weights[t] * (dprobs[:, t * BLK : (t + 1) * BLK] - delta)).astype(jnp.bfloat16)
                    for t in range(tiles)
                ],
                axis=1,
            )
            grad2 = jnp.dot(dscores, keys, preferred_element_type=jnp.float32)
            grad_q_ref[rows, cols] = (unstack_heads(grad2, low) * scale).astype(jnp.bfloat16)
            for which, product in ((0, dot_first(dscores, q2)), (1, dot_first(weights_low, g2))):
                local_ref[which, rows, cols] = product[:BLK]
                for t in range(1, tiles):
                    j = slots[t - 1]
                    held = parts_ref[j, which, :, cols].astype(jnp.float32)
                    parts_ref[j, which, :, cols] = (
                        held + product[t * BLK : (t + 1) * BLK]
                    ).astype(jnp.bfloat16)


def attention(axis_length, frames, sink, queries, keys_values, cotangent, anchors):
    vmem = pl.BlockSpec(memory_space=pltpu.VMEM)
    smem = pl.BlockSpec(memory_space=pltpu.SMEM)
    return pl.pallas_call(
        functools.partial(attention_kernel, axis_length),
        out_shape=(
            jax.ShapeDtypeStruct(queries.shape, jnp.bfloat16),
            jax.ShapeDtypeStruct(queries.shape, jnp.bfloat16),
            jax.ShapeDtypeStruct(keys_values.shape, jnp.float32),
            jax.ShapeDtypeStruct(anchors.shape, jnp.bfloat16),
        ),
        in_specs=[smem, smem, vmem, vmem, vmem, vmem],
        out_specs=[vmem] * 4,
        compiler_params=pltpu.CompilerParams(vmem_limit_bytes=VMEM_BYTES),
        name="attention",
    )(frames, sink, queries, keys_values, cotangent, anchors)


def gather_kernel(
    axis_length, y_count, kv_ref, out_ref, own_sem, up_sem, down_sem, y_sem, core_sem, recv_sem
):
    z_count = axis_length // (2 * y_count)
    me = lax.axis_index("seq")
    core = me % 2
    y = (me // 2) % y_count
    z = me // (2 * y_count)
    y_peer = (z * y_count + (y_count - 1 - y)) * 2 + core
    sibling = me + 1 - 2 * core
    offset = core * BLK

    def index(z_at, y_at, core_at):
        return (z_at * y_count + y_at) * 2 + core_at

    barrier = pltpu.get_barrier_semaphore()

    for k in range(1, z_count):
        pl.semaphore_signal(
            barrier, inc=1, device_id={"seq": index((z + k) % z_count, y, core)}
        )
    peers = z_count
    pl.semaphore_signal(barrier, inc=1, device_id={"seq": sibling})
    if y_count > 1:
        pl.semaphore_signal(barrier, inc=1, device_id={"seq": y_peer})
        peers += 1
    pl.semaphore_wait(barrier, peers)

    def remote(piece, which, target, send_sem, own=False):
        place = out_ref.at[piece, which]
        source = kv_ref.at[which, pl.ds(offset, BLK)] if own else place
        return pltpu.make_async_remote_copy(
            src_ref=source,
            dst_ref=place,
            send_sem=send_sem,
            recv_sem=recv_sem.at[piece, which],
            device_id={"seq": target},
            device_id_type=pl.DeviceIdType.MESH,
        )

    def await_piece(piece, which):
        remote(piece, which, sibling, core_sem.at[0, which]).wait_recv()

    def to_up(step, which, own=False):
        return remote(
            index(z - step, y, core), which, me + 2 * y_count, up_sem.at[step, which], own
        )

    def to_down(step, which, own=False):
        return remote(
            index(z + step, y, core), which, me - 2 * y_count, down_sem.at[step, which], own
        )

    def to_y(z_at, which, own=False):
        return remote(index(z_at, y, core), which, y_peer, y_sem.at[z_at, which], own)

    def to_core(z_at, y_at, which, own=False):
        return remote(
            index(z_at, y_at, core), which, sibling, core_sem.at[z_at * y_count + y_at, which], own
        )

    def own_copy(which):
        return pltpu.make_async_copy(
            kv_ref.at[which, pl.ds(offset, BLK)], out_ref.at[me, which], own_sem.at[which]
        )

    for which in range(2):
        pl.when(z < z_count - 1)(lambda: to_up(0, which, True).start())
        pl.when(z > 0)(lambda: to_down(0, which, True).start())
        if y_count > 1:
            to_y(z, which, True).start()
        to_core(z, y, which, True).start()
    for which in range(2):
        own_copy(which).start()

    def pass_y(distance):
        if y_count == 1:
            return
        for which in range(2):
            def hand(z_at):
                await_piece(index(z_at, 1 - y, core), which)
                to_core(z_at, 1 - y, which).start()

            pl.when(z - distance >= 0)(lambda: hand(z - distance))
            if distance:
                pl.when(z + distance < z_count)(lambda: hand(z + distance))

    for step in range(1, z_count):
        for which in range(2):
            @pl.when(z - step >= 0)
            def _():
                await_piece(index(z - step, y, core), which)
                pl.when(z < z_count - 1)(lambda: to_up(step, which).start())
                if y_count > 1:
                    to_y(z - step, which).start()
                to_core(z - step, y, which).start()

            @pl.when(z + step < z_count)
            def _():
                await_piece(index(z + step, y, core), which)
                pl.when(z > 0)(lambda: to_down(step, which).start())
                if y_count > 1:
                    to_y(z + step, which).start()
                to_core(z + step, y, which).start()
        pass_y(step - 1)
    pass_y(z_count - 1)

    for which in range(2):
        own_copy(which).wait()
        for z_at in range(z_count):
            for y_at in range(y_count):
                await_piece(index(z_at, y_at, 1 - core), which)
        for z_at in range(z_count):
            if y_count > 1:
                to_y(z_at, which).wait_send()
            for y_at in range(y_count):
                to_core(z_at, y_at, which).wait_send()
            pl.when((z - z_at >= 0) & (z < z_count - 1))(lambda: to_up(z_at, which).wait_send())
            pl.when((z + z_at < z_count) & (z > 0))(lambda: to_down(z_at, which).wait_send())


def gather_anchors(axis_length, y_count, keys_values):
    z_count = axis_length // (2 * y_count)
    hbm = pl.BlockSpec(memory_space=pl.ANY)
    dma = pltpu.SemaphoreType.DMA
    return pl.pallas_call(
        functools.partial(gather_kernel, axis_length, y_count),
        out_shape=jax.ShapeDtypeStruct(
            (axis_length, 2, BLK, keys_values.shape[2]), jnp.bfloat16
        ),
        in_specs=[hbm],
        out_specs=hbm,
        scratch_shapes=[
            dma((2,)),
            dma((z_count, 2)),
            dma((z_count, 2)),
            dma((z_count, 2)),
            dma((z_count * y_count, 2)),
            dma((axis_length, 2)),
        ],
        compiler_params=pltpu.CompilerParams(collective_id=0, has_side_effects=True),
        name="gather",
    )(keys_values)


def reduce_kernel(
    axis_length,
    y_count,
    local_ref,
    parts_ref,
    out_ref,
    from_core,
    from_y,
    from_z,
    core_sum,
    z_term,
    core_send,
    core_recv,
    y_send,
    y_recv,
    z_send,
    z_recv,
):
    z_count = axis_length // (2 * y_count)
    me = lax.axis_index("seq")
    core = me % 2
    y = (me // 2) % y_count
    z = me // (2 * y_count)
    other_y = y_count - 1 - y
    y_peer = (z * y_count + other_y) * 2 + core
    sibling = me + 1 - 2 * core
    offset = core * BLK
    stride = jnp.where(z < z_count // 2, -1, 1)
    order = [(z + stride * (1 + k) + z_count) % z_count for k in range(z_count)]

    barrier = pltpu.get_barrier_semaphore()
    peers = z_count - 1 + y_count
    for k in range(z_count - 1):
        pl.semaphore_signal(
            barrier, inc=1, device_id={"seq": (order[k] * y_count + y) * 2 + core}
        )
    pl.semaphore_signal(barrier, inc=1, device_id={"seq": sibling})
    if y_count > 1:
        pl.semaphore_signal(barrier, inc=1, device_id={"seq": y_peer})
    pl.semaphore_wait(barrier, peers)

    def remote(source, place, send_sem, recv_sem, target):
        return pltpu.make_async_remote_copy(
            src_ref=source,
            dst_ref=place,
            send_sem=send_sem,
            recv_sem=recv_sem,
            device_id={"seq": target},
            device_id_type=pl.DeviceIdType.MESH,
        )

    def to_core(piece):
        return remote(
            parts_ref.at[piece * 2 + 1 - core],
            from_core.at[piece],
            core_send.at[piece],
            core_recv.at[piece],
            sibling,
        )

    def to_y(k, which):
        return remote(
            core_sum.at[order[k] * y_count + other_y, which],
            from_y.at[order[k], which],
            y_send.at[k, which],
            y_recv.at[k, which],
            y_peer,
        )

    def to_z(k, which):
        return remote(
            z_term.at[order[k], which],
            from_z.at[z, which],
            z_send.at[k, which],
            z_recv.at[z, which],
            (order[k] * y_count + y) * 2 + core,
        )

    def from_z_wait(k, which):
        remote(
            z_term.at[order[k], which],
            from_z.at[order[k], which],
            z_send.at[k, which],
            z_recv.at[order[k], which],
            sibling,
        ).wait_recv()

    def wide(value):
        return value.astype(jnp.float32)

    def merge_core(piece):
        to_core(piece).wait_recv()
        for which in range(2):
            core_sum[piece, which] = (
                wide(parts_ref[piece * 2 + core, which]) + wide(from_core[piece, which])
            ).astype(jnp.bfloat16)

    if y_count > 1:
        for k in range(z_count):
            to_core(order[k] * y_count + other_y).start()
    for k in range(z_count):
        to_core(order[k] * y_count + y).start()
    if y_count > 1:
        for k in range(z_count):
            merge_core(order[k] * y_count + other_y)
            for which in range(2):
                to_y(k, which).start()
    for k in range(z_count):
        merge_core(order[k] * y_count + y)
    rest = (1 - core) * BLK
    for which in range(2):
        out_ref[which, pl.ds(rest, BLK)] = local_ref[which, pl.ds(rest, BLK)].astype(jnp.bfloat16)
    for k in range(z_count):
        for which in range(2):
            term = wide(core_sum[order[k] * y_count + y, which])
            if y_count > 1:
                to_y(k, which).wait_recv()
                term = term + wide(from_y[order[k], which])
            if k < z_count - 1:
                z_term[order[k], which] = term.astype(jnp.bfloat16)
                to_z(k, which).start()
            else:
                total = term + local_ref[which, pl.ds(offset, BLK)]
                for other in range(z_count - 1):
                    from_z_wait(other, which)
                    total = total + wide(from_z[order[other], which])
                out_ref[which, pl.ds(offset, BLK)] = total.astype(jnp.bfloat16)
    for k in range(z_count):
        for y_at in range(y_count):
            to_core(order[k] * y_count + y_at).wait_send()
        for which in range(2):
            if y_count > 1:
                to_y(k, which).wait_send()
            if k < z_count - 1:
                to_z(k, which).wait_send()


def reduce_parts(axis_length, y_count, local, parts):
    z_count = axis_length // (2 * y_count)
    chips = axis_length // 2
    tile = parts.shape[1:]
    vmem = pl.BlockSpec(memory_space=pltpu.VMEM)
    dma = pltpu.SemaphoreType.DMA
    return pl.pallas_call(
        functools.partial(reduce_kernel, axis_length, y_count),
        out_shape=jax.ShapeDtypeStruct(local.shape, jnp.bfloat16),
        in_specs=[vmem, vmem],
        out_specs=vmem,
        scratch_shapes=[
            pltpu.VMEM((chips,) + tile, jnp.bfloat16),
            pltpu.VMEM((z_count,) + tile, jnp.bfloat16),
            pltpu.VMEM((z_count,) + tile, jnp.bfloat16),
            pltpu.VMEM((chips,) + tile, jnp.bfloat16),
            pltpu.VMEM((z_count,) + tile, jnp.bfloat16),
            dma((chips,)),
            dma((chips,)),
            dma((z_count, 2)),
            dma((z_count, 2)),
            dma((z_count, 2)),
            dma((z_count, 2)),
        ],
        compiler_params=pltpu.CompilerParams(
            collective_id=1, has_side_effects=True, vmem_limit_bytes=VMEM_BYTES
        ),
        name="reduce",
    )(local, parts)


def shards(y_count, queries, keys_values, cotangent, frame_lists, sink_owner):
    axis_length = lax.axis_size("seq")
    anchors = gather_anchors(axis_length, y_count, keys_values)
    attended, grad_queries, local, parts = attention(
        axis_length, frame_lists, sink_owner, queries, keys_values, cotangent, anchors
    )
    return attended, grad_queries, reduce_parts(axis_length, y_count, local, parts)


def solution(mesh):
    rows = P(("groups", "seq"), None)
    pairs = P(None, ("groups", "seq"), None)
    y_count = 2 if mesh.shape["groups"] == 2 and mesh.shape["seq"] % 4 == 0 else 1
    return jax.shard_map(
        functools.partial(shards, y_count),
        mesh=mesh,
        in_specs=(rows, pairs, rows, rows, P("groups")),
        out_specs=(rows, rows, pairs),
        check_vma=False,
    )
```

```python
import functools
import math

import jax
import jax.numpy as jnp
from jax import lax
from jax.experimental import pallas as pl
from jax.experimental.pallas import tpu as pltpu
from jax.sharding import PartitionSpec as P

HEAD = 64
BLK = 128
PAIR = 2 * HEAD
NEG = -1e30
VMEM_BYTES = 60 * 1024 * 1024


def anchor_span(device_id, axis_length):
    return jnp.where(device_id % 2 == 0, device_id, 2 * axis_length - 1 - device_id)


def stack_heads(rows, low):
    zero = jnp.zeros_like(rows)
    return jnp.concatenate((jnp.where(low, rows, zero), jnp.where(low, zero, rows)), axis=0)


def unstack_heads(rows, low):
    return jnp.where(low, rows[:BLK], rows[BLK:])


def dot_last(left, right):
    return lax.dot_general(left, right, (((1,), (1,)), ((), ())), preferred_element_type=jnp.float32)


def dot_first(left, right):
    return lax.dot_general(left, right, (((0,), (0,)), ((), ())), preferred_element_type=jnp.float32)


def attend_step(
    axis_length, half, item, frames_ref, sink_ref, q_ref, kv_ref, g_ref, anchors_ref, outs
):
    out_ref, grad_q_ref, local_ref, entry_ref = outs
    me = lax.axis_index("seq")
    sink = sink_ref[0]
    entries = frames_ref.shape[1]
    pairs = anchors_ref.shape[3] // PAIR
    scale = 1.0 / math.sqrt(HEAD)
    low = lax.broadcasted_iota(jnp.int32, (BLK, PAIR), 1) < HEAD
    row = lax.broadcasted_iota(jnp.int32, (2 * BLK, BLK), 0) % BLK
    causal = lax.broadcasted_iota(jnp.int32, (2 * BLK, BLK), 1) <= row
    block = jnp.where(item >= pairs, 1, 0)
    pair = item - block * pairs
    span = jnp.where(block == 0, me, 2 * axis_length - 1 - me)
    rows = pl.ds(pl.multiple_of(block * BLK, BLK), BLK)
    ids = [frames_ref[block, e] for e in range(entries)]
    biases = []
    for e in range(entries):
        valid = (anchor_span(ids[e], axis_length) < span) & (ids[e] != sink)
        for earlier in range(e):
            valid = valid & (ids[e] != ids[earlier])
        biases.append(jnp.where(valid, 0.0, NEG))
    slots = ids + [sink]
    window_scalar = jnp.where(span == anchor_span(sink, axis_length), NEG, 0.0)
    window_bias = jnp.where(causal, window_scalar, NEG)
    cols = pl.ds(pl.multiple_of((half * pairs + pair) * PAIR, PAIR), PAIR)
    near = pl.ds(pl.multiple_of(pair * PAIR, PAIR), PAIR)
    out_cols = cols if out_ref.shape[1] == q_ref.shape[1] else near
    q2 = stack_heads(q_ref[rows, cols] * jnp.bfloat16(scale), low)
    grad = g_ref[rows, cols]
    g2 = stack_heads(grad, low)
    keys = jnp.concatenate(
        [kv_ref[0, rows, cols]] + [anchors_ref[j, 0, :, near] for j in slots], axis=0
    )
    values = jnp.concatenate(
        [kv_ref[1, rows, cols]] + [anchors_ref[j, 1, :, near] for j in slots], axis=0
    )
    tiles = 1 + len(slots)
    scores = dot_last(q2, keys)
    parts = [scores[:, t * BLK : (t + 1) * BLK] for t in range(tiles)]
    parts[0] = parts[0] + window_bias
    for t in range(1, tiles - 1):
        parts[t] = parts[t] + biases[t - 1]
    top = functools.reduce(jnp.maximum, parts)
    top = jnp.max(top, axis=1, keepdims=True)
    weights = [jnp.exp(part - top) for part in parts]
    total = jnp.sum(functools.reduce(jnp.add, weights), axis=1, keepdims=True)
    inverse = 1.0 / total
    weights = [w * inverse for w in weights]
    weights_low = jnp.concatenate([w.astype(jnp.bfloat16) for w in weights], axis=1)
    out2 = jnp.dot(weights_low, values, preferred_element_type=jnp.float32)
    attended = unstack_heads(out2, low).astype(jnp.bfloat16)
    out_ref[rows, out_cols] = attended
    product = grad.astype(jnp.float32) * attended.astype(jnp.float32)
    delta = jnp.sum(stack_heads(product, low), axis=1, keepdims=True)
    dprobs = dot_last(g2, values)
    dscores = jnp.concatenate(
        [
            (weights[t] * (dprobs[:, t * BLK : (t + 1) * BLK] - delta)).astype(jnp.bfloat16)
            for t in range(tiles)
        ],
        axis=1,
    )
    grad2 = jnp.dot(dscores, keys, preferred_element_type=jnp.float32)
    grad_q_ref[rows, out_cols] = (unstack_heads(grad2, low) * scale).astype(jnp.bfloat16)
    for which, product in ((0, dot_first(dscores, q2)), (1, dot_first(weights_low, g2))):
        local_ref[which, rows, near] = product[:BLK]
        for t in range(1, tiles):
            entry_ref[block, t - 1, which, :, near] = product[t * BLK : (t + 1) * BLK].astype(
                jnp.bfloat16
            )


def clear_entries(entry_ref, entries):
    for block in range(2):
        entry_ref[block, entries + 1] = jnp.zeros(entry_ref.shape[2:], jnp.bfloat16)


def assemble(axis_length, frames_ref, sink_ref, entry_ref, parts_ref):
    entries = frames_ref.shape[1]

    @pl.loop(0, axis_length)
    def _(j):
        picked = []
        for block in range(2):
            slot = entries + 1
            for e in reversed(range(entries)):
                slot = jnp.where(frames_ref[block, e] == j, e, slot)
            picked.append(jnp.where(sink_ref[0] == j, entries, slot))
        for which in range(2):
            parts_ref[j, which] = (
                entry_ref[0, picked[0], which].astype(jnp.float32)
                + entry_ref[1, picked[1], which].astype(jnp.float32)
            ).astype(jnp.bfloat16)


def gather_attend_kernel(
    axis_length,
    y_count,
    frames_ref,
    sink_ref,
    q_ref,
    kv_ref,
    g_ref,
    out_ref,
    grad_q_ref,
    local_ref,
    parts_ref,
    second_ref,
    first_ref,
    entry_ref,
    own_sem,
    up_sem,
    down_sem,
    y_sem,
    core_sem,
    recv_sem,
):
    z_count = axis_length // (2 * y_count)
    me = lax.axis_index("seq")
    core = me % 2
    y = (me // 2) % y_count
    z = me // (2 * y_count)
    y_peer = (z * y_count + (y_count - 1 - y)) * 2 + core
    sibling = me + 1 - 2 * core
    offset = core * BLK
    width = first_ref.shape[3]
    items = 2 * width // PAIR
    step_items = -(-items // (z_count - 1))

    def index(z_at, y_at, core_at):
        return (z_at * y_count + y_at) * 2 + core_at

    barrier = pltpu.get_barrier_semaphore()

    for k in range(1, z_count):
        pl.semaphore_signal(
            barrier, inc=1, device_id={"seq": index((z + k) % z_count, y, core)}
        )
    peers = z_count
    pl.semaphore_signal(barrier, inc=1, device_id={"seq": sibling})
    if y_count > 1:
        pl.semaphore_signal(barrier, inc=1, device_id={"seq": y_peer})
        peers += 1
    pl.semaphore_wait(barrier, peers)

    def plan(half, buffer):
        def remote(piece, which, target, send_sem, own=False):
            place = buffer.at[piece, which]
            source = kv_ref.at[which, pl.ds(offset, BLK), pl.ds(half * width, width)] if own else place
            return pltpu.make_async_remote_copy(
                src_ref=source,
                dst_ref=place,
                send_sem=send_sem,
                recv_sem=recv_sem.at[half, piece, which],
                device_id={"seq": target},
                device_id_type=pl.DeviceIdType.MESH,
            )

        def await_piece(piece, which):
            remote(piece, which, sibling, core_sem.at[half, 0, which]).wait_recv()

        def to_up(step, which, own=False):
            return remote(
                index(z - step, y, core), which, me + 2 * y_count, up_sem.at[half, step, which], own
            )

        def to_down(step, which, own=False):
            return remote(
                index(z + step, y, core), which, me - 2 * y_count, down_sem.at[half, step, which], own
            )

        def to_y(z_at, which, own=False):
            return remote(index(z_at, y, core), which, y_peer, y_sem.at[half, z_at, which], own)

        def to_core(z_at, y_at, which, own=False):
            return remote(
                index(z_at, y_at, core), which, sibling, core_sem.at[half, z_at * y_count + y_at, which], own
            )

        def own_copy(which):
            return pltpu.make_async_copy(
                kv_ref.at[which, pl.ds(offset, BLK), pl.ds(half * width, width)], buffer.at[me, which], own_sem.at[half, which]
            )

        def begin():
            for which in range(2):
                pl.when(z < z_count - 1)(lambda: to_up(0, which, True).start())
                pl.when(z > 0)(lambda: to_down(0, which, True).start())
                if y_count > 1:
                    to_y(z, which, True).start()
                to_core(z, y, which, True).start()
            for which in range(2):
                own_copy(which).start()

        def pass_y(distance):
            if y_count == 1:
                return
            for which in range(2):
                def hand(z_at):
                    await_piece(index(z_at, 1 - y, core), which)
                    to_core(z_at, 1 - y, which).start()

                pl.when(z - distance >= 0)(lambda: hand(z - distance))
                if distance:
                    pl.when(z + distance < z_count)(lambda: hand(z + distance))

        def pass_step(step):
            for which in range(2):
                @pl.when(z - step >= 0)
                def _():
                    await_piece(index(z - step, y, core), which)
                    pl.when(z < z_count - 1)(lambda: to_up(step, which).start())
                    if y_count > 1:
                        to_y(z - step, which).start()
                    to_core(z - step, y, which).start()

                @pl.when(z + step < z_count)
                def _():
                    await_piece(index(z + step, y, core), which)
                    pl.when(z > 0)(lambda: to_down(step, which).start())
                    if y_count > 1:
                        to_y(z + step, which).start()
                    to_core(z + step, y, which).start()
            pass_y(step - 1)
        def arrive():
            for which in range(2):
                own_copy(which).wait()
                for z_at in range(z_count):
                    for y_at in range(y_count):
                        await_piece(index(z_at, y_at, 1 - core), which)
        def finish():
            for which in range(2):
                for z_at in range(z_count):
                    if y_count > 1:
                        to_y(z_at, which).wait_send()
                    for y_at in range(y_count):
                        to_core(z_at, y_at, which).wait_send()
                    pl.when((z - z_at >= 0) & (z < z_count - 1))(lambda: to_up(z_at, which).wait_send())
                    pl.when((z + z_at < z_count) & (z > 0))(lambda: to_down(z_at, which).wait_send())


        return begin, pass_step, pass_y, arrive, finish

    def work(low_item, high_item):
        @pl.loop(low_item, high_item)
        def _(item):
            attend_step(
                axis_length, 0, item, frames_ref, sink_ref, q_ref, kv_ref, g_ref, first_ref,
                (out_ref, grad_q_ref, local_ref, entry_ref),
            )

    begin, pass_step, pass_y, arrive, finish = plan(0, first_ref)
    begin_second, pass_step_second, pass_y_second, arrive_second, finish_second = plan(
        1, second_ref
    )
    begin()
    clear_entries(entry_ref, frames_ref.shape[1])
    for step in range(1, z_count):
        pass_step(step)
    begin_second()
    pass_y(z_count - 1)
    arrive()
    done = 0
    for step in range(1, z_count):
        pass_step_second(step)
        upto = min(items, done + step_items)
        if upto > done:
            work(done, upto)
        done = upto
    pass_y_second(z_count - 1)
    assemble(axis_length, frames_ref, sink_ref, entry_ref, parts_ref)
    arrive_second()
    finish()
    finish_second()


def gather_attend(axis_length, y_count, frames, sink, queries, keys_values, cotangent):
    z_count = axis_length // (2 * y_count)
    rows, width = queries.shape
    half = width // 2
    entries = frames.shape[1]
    vmem = pl.BlockSpec(memory_space=pltpu.VMEM)
    smem = pl.BlockSpec(memory_space=pltpu.SMEM)
    hbm = pl.BlockSpec(memory_space=pl.ANY)
    dma = pltpu.SemaphoreType.DMA
    gathered = (axis_length, 2, BLK, half)
    return pl.pallas_call(
        functools.partial(gather_attend_kernel, axis_length, y_count),
        out_shape=(
            jax.ShapeDtypeStruct((rows, half), jnp.bfloat16),
            jax.ShapeDtypeStruct((rows, half), jnp.bfloat16),
            jax.ShapeDtypeStruct((2, rows, half), jnp.float32),
            jax.ShapeDtypeStruct(gathered, jnp.bfloat16),
            jax.ShapeDtypeStruct(gathered, jnp.bfloat16),
        ),
        in_specs=[smem, smem, vmem, vmem, vmem],
        out_specs=[vmem, vmem, vmem, vmem, hbm],
        scratch_shapes=[
            pltpu.VMEM(gathered, jnp.bfloat16),
            pltpu.VMEM((2, entries + 2, 2, BLK, half), jnp.bfloat16),
            dma((2, 2)),
            dma((2, z_count, 2)),
            dma((2, z_count, 2)),
            dma((2, z_count, 2)),
            dma((2, z_count * y_count, 2)),
            dma((2, axis_length, 2)),
        ],
        compiler_params=pltpu.CompilerParams(
            collective_id=0, has_side_effects=True, vmem_limit_bytes=VMEM_BYTES
        ),
        name="gather_attend",
    )(frames, sink, queries, keys_values, cotangent)


def attend_reduce_kernel(
    axis_length,
    y_count,
    frames_ref,
    sink_ref,
    q_ref,
    kv_ref,
    g_ref,
    anchors_ref,
    first_out_ref,
    first_grad_ref,
    first_local_ref,
    first_parts_ref,
    attended_ref,
    grad_q_ref,
    grad_kv_ref,
    second_local_ref,
    second_parts_ref,
    entry_ref,
    from_core,
    from_y,
    from_z,
    core_sum,
    z_term,
    core_send,
    core_recv,
    y_send,
    y_recv,
    z_send,
    z_recv,
):
    z_count = axis_length // (2 * y_count)
    me = lax.axis_index("seq")
    core = me % 2
    y = (me // 2) % y_count
    z = me // (2 * y_count)
    other_y = y_count - 1 - y
    y_peer = (z * y_count + other_y) * 2 + core
    sibling = me + 1 - 2 * core
    offset = core * BLK
    rest = (1 - core) * BLK
    width = anchors_ref.shape[3]
    items = 2 * width // PAIR
    step_items = -(-items // (z_count - 1))
    stride = jnp.where(z < z_count // 2, -1, 1)
    order = [(z + stride * (1 + k) + z_count) % z_count for k in range(z_count)]

    barrier = pltpu.get_barrier_semaphore()
    peers = z_count - 1 + y_count
    for k in range(z_count - 1):
        pl.semaphore_signal(
            barrier, inc=1, device_id={"seq": (order[k] * y_count + y) * 2 + core}
        )
    pl.semaphore_signal(barrier, inc=1, device_id={"seq": sibling})
    if y_count > 1:
        pl.semaphore_signal(barrier, inc=1, device_id={"seq": y_peer})
    pl.semaphore_wait(barrier, peers)

    def plan(half, local_ref, parts_ref):
        def remote(source, place, send_sem, recv_sem, target):
            return pltpu.make_async_remote_copy(
                src_ref=source,
                dst_ref=place,
                send_sem=send_sem,
                recv_sem=recv_sem,
                device_id={"seq": target},
                device_id_type=pl.DeviceIdType.MESH,
            )

        def to_core(piece):
            return remote(
                parts_ref.at[piece * 2 + 1 - core],
                from_core.at[half, piece],
                core_send.at[half, piece],
                core_recv.at[half, piece],
                sibling,
            )

        def to_y(k, which):
            return remote(
                core_sum.at[half, order[k] * y_count + other_y, which],
                from_y.at[half, order[k], which],
                y_send.at[half, k, which],
                y_recv.at[half, k, which],
                y_peer,
            )

        def to_z(k, which):
            return remote(
                z_term.at[half, order[k], which],
                from_z.at[half, z, which],
                z_send.at[half, k, which],
                z_recv.at[half, z, which],
                (order[k] * y_count + y) * 2 + core,
            )

        def from_z_wait(k, which):
            remote(
                z_term.at[half, order[k], which],
                from_z.at[half, order[k], which],
                z_send.at[half, k, which],
                z_recv.at[half, order[k], which],
                sibling,
            ).wait_recv()

        def wide(value):
            return value.astype(jnp.float32)

        def merge_core(piece):
            to_core(piece).wait_recv()
            for which in range(2):
                core_sum[half, piece, which] = (
                    wide(parts_ref[piece * 2 + core, which]) + wide(from_core[half, piece, which])
                ).astype(jnp.bfloat16)

        def begin():
            if y_count > 1:
                for k in range(z_count):
                    to_core(order[k] * y_count + other_y).start()
            for k in range(z_count):
                to_core(order[k] * y_count + y).start()
            if y_count > 1:
                for k in range(z_count):
                    merge_core(order[k] * y_count + other_y)
                    for which in range(2):
                        to_y(k, which).start()
            for k in range(z_count):
                merge_core(order[k] * y_count + y)

        def term_of(k, which):
            term = wide(core_sum[half, order[k] * y_count + y, which])
            if y_count > 1:
                to_y(k, which).wait_recv()
                term = term + wide(from_y[half, order[k], which])
            return term

        def pass_z(k):
            for which in range(2):
                z_term[half, order[k], which] = term_of(k, which).astype(jnp.bfloat16)
                to_z(k, which).start()

        def total():
            cols = pl.ds(half * width, width)
            for which in range(2):
                grad_kv_ref[which, pl.ds(rest, BLK), cols] = local_ref[
                    which, pl.ds(rest, BLK)
                ].astype(jnp.bfloat16)
                summed = term_of(z_count - 1, which) + local_ref[which, pl.ds(offset, BLK)]
                for other in range(z_count - 1):
                    from_z_wait(other, which)
                    summed = summed + wide(from_z[half, order[other], which])
                grad_kv_ref[which, pl.ds(offset, BLK), cols] = summed.astype(jnp.bfloat16)

        def finish():
            for k in range(z_count):
                for y_at in range(y_count):
                    to_core(order[k] * y_count + y_at).wait_send()
                for which in range(2):
                    if y_count > 1:
                        to_y(k, which).wait_send()
                    if k < z_count - 1:
                        to_z(k, which).wait_send()

        return begin, pass_z, total, finish

    def work(low_item, high_item):
        @pl.loop(low_item, high_item)
        def _(item):
            attend_step(
                axis_length, 1, item, frames_ref, sink_ref, q_ref, kv_ref, g_ref, anchors_ref,
                (attended_ref, grad_q_ref, second_local_ref, entry_ref),
            )

    begin, pass_z, total, finish = plan(0, first_local_ref, first_parts_ref)
    begin_second, pass_z_second, total_second, finish_second = plan(
        1, second_local_ref, second_parts_ref
    )
    begin()
    clear_entries(entry_ref, frames_ref.shape[1])
    attended_ref[:, pl.ds(0, width)] = first_out_ref[...]
    grad_q_ref[:, pl.ds(0, width)] = first_grad_ref[...]
    done = 0
    for k in range(z_count - 1):
        upto = min(items, done + step_items)
        if upto > done:
            work(done, upto)
        done = upto
        pass_z(k)
    assemble(axis_length, frames_ref, sink_ref, entry_ref, second_parts_ref)
    begin_second()
    total()
    for k in range(z_count - 1):
        pass_z_second(k)
    total_second()
    finish()
    finish_second()


def attend_reduce(axis_length, y_count, frames, sink, queries, keys_values, cotangent, gathered):
    attended, grad_queries, local, parts, anchors = gathered
    z_count = axis_length // (2 * y_count)
    chips = axis_length // 2
    tile = parts.shape[1:]
    entries = frames.shape[1]
    vmem = pl.BlockSpec(memory_space=pltpu.VMEM)
    smem = pl.BlockSpec(memory_space=pltpu.SMEM)
    dma = pltpu.SemaphoreType.DMA
    return pl.pallas_call(
        functools.partial(attend_reduce_kernel, axis_length, y_count),
        out_shape=(
            jax.ShapeDtypeStruct(queries.shape, jnp.bfloat16),
            jax.ShapeDtypeStruct(queries.shape, jnp.bfloat16),
            jax.ShapeDtypeStruct(keys_values.shape, jnp.bfloat16),
        ),
        in_specs=[smem, smem] + [vmem] * 8,
        out_specs=[vmem] * 3,
        scratch_shapes=[
            pltpu.VMEM(local.shape, jnp.float32),
            pltpu.VMEM(parts.shape, jnp.bfloat16),
            pltpu.VMEM((2, entries + 2) + tile, jnp.bfloat16),
            pltpu.VMEM((2, chips) + tile, jnp.bfloat16),
            pltpu.VMEM((2, z_count) + tile, jnp.bfloat16),
            pltpu.VMEM((2, z_count) + tile, jnp.bfloat16),
            pltpu.VMEM((2, chips) + tile, jnp.bfloat16),
            pltpu.VMEM((2, z_count) + tile, jnp.bfloat16),
            dma((2, chips)),
            dma((2, chips)),
            dma((2, z_count, 2)),
            dma((2, z_count, 2)),
            dma((2, z_count, 2)),
            dma((2, z_count, 2)),
        ],
        compiler_params=pltpu.CompilerParams(
            collective_id=1, has_side_effects=True, vmem_limit_bytes=VMEM_BYTES
        ),
        name="attend_reduce",
    )(
        frames, sink, queries, keys_values, cotangent, anchors,
        attended, grad_queries, local, parts,
    )


def shards(y_count, queries, keys_values, cotangent, frame_lists, sink_owner):
    axis_length = lax.axis_size("seq")
    args = (axis_length, y_count, frame_lists, sink_owner, queries, keys_values, cotangent)
    return attend_reduce(*args, gather_attend(*args))


def solution(mesh):
    rows = P(("groups", "seq"), None)
    pairs = P(None, ("groups", "seq"), None)
    y_count = 2 if mesh.shape["groups"] == 2 and mesh.shape["seq"] % 4 == 0 else 1
    return jax.shard_map(
        functools.partial(shards, y_count),
        mesh=mesh,
        in_specs=(rows, pairs, rows, rows, P("groups")),
        out_specs=(rows, rows, pairs),
        check_vma=False,
    )
```

```python
import functools
import math

import jax
import jax.numpy as jnp
from jax import lax
from jax.experimental import pallas as pl
from jax.experimental.pallas import tpu as pltpu
from jax.sharding import PartitionSpec as P

HEAD = 64
BLK = 128
PAIR = 2 * HEAD
NEG = -1e30
VMEM_BYTES = 60 * 1024 * 1024


def anchor_span(device_id, axis_length):
    return jnp.where(device_id % 2 == 0, device_id, 2 * axis_length - 1 - device_id)


def stack_heads(rows, low):
    zero = jnp.zeros_like(rows)
    return jnp.concatenate((jnp.where(low, rows, zero), jnp.where(low, zero, rows)), axis=0)


def unstack_heads(rows, low):
    return jnp.where(low, rows[:BLK], rows[BLK:])


def dot_last(left, right):
    return lax.dot_general(left, right, (((1,), (1,)), ((), ())), preferred_element_type=jnp.float32)


def dot_first(left, right):
    return lax.dot_general(left, right, (((0,), (0,)), ((), ())), preferred_element_type=jnp.float32)


def attend_step(
    axis_length, half, item, frames_ref, sink_ref, q_ref, kv_ref, g_ref, anchors_ref, outs
):
    out_ref, grad_q_ref, local_ref, entry_ref = outs
    me = lax.axis_index("seq")
    sink = sink_ref[0]
    entries = frames_ref.shape[1]
    pairs = anchors_ref.shape[3] // PAIR
    scale = 1.0 / math.sqrt(HEAD)
    low = lax.broadcasted_iota(jnp.int32, (BLK, PAIR), 1) < HEAD
    row = lax.broadcasted_iota(jnp.int32, (2 * BLK, BLK), 0) % BLK
    causal = lax.broadcasted_iota(jnp.int32, (2 * BLK, BLK), 1) <= row
    block = jnp.where(item >= pairs, 1, 0)
    pair = item - block * pairs
    span = jnp.where(block == 0, me, 2 * axis_length - 1 - me)
    rows = pl.ds(pl.multiple_of(block * BLK, BLK), BLK)
    ids = [frames_ref[block, e] for e in range(entries)]
    biases = []
    for e in range(entries):
        valid = (anchor_span(ids[e], axis_length) < span) & (ids[e] != sink)
        for earlier in range(e):
            valid = valid & (ids[e] != ids[earlier])
        biases.append(jnp.where(valid, 0.0, NEG))
    slots = ids + [sink]
    window_scalar = jnp.where(span == anchor_span(sink, axis_length), NEG, 0.0)
    window_bias = jnp.where(causal, window_scalar, NEG)
    cols = pl.ds(pl.multiple_of((half * pairs + pair) * PAIR, PAIR), PAIR)
    near = pl.ds(pl.multiple_of(pair * PAIR, PAIR), PAIR)
    out_cols = cols if out_ref.shape[1] == q_ref.shape[1] else near
    q2 = stack_heads(q_ref[rows, cols] * jnp.bfloat16(scale), low)
    grad = g_ref[rows, cols]
    g2 = stack_heads(grad, low)
    keys = jnp.concatenate(
        [kv_ref[0, rows, cols]] + [anchors_ref[j, 0, :, near] for j in slots], axis=0
    )
    values = jnp.concatenate(
        [kv_ref[1, rows, cols]] + [anchors_ref[j, 1, :, near] for j in slots], axis=0
    )
    tiles = 1 + len(slots)
    scores = dot_last(q2, keys)
    parts = [scores[:, t * BLK : (t + 1) * BLK] for t in range(tiles)]
    parts[0] = parts[0] + window_bias
    for t in range(1, tiles - 1):
        parts[t] = parts[t] + biases[t - 1]
    top = functools.reduce(jnp.maximum, parts)
    top = jnp.max(top, axis=1, keepdims=True)
    weights = [jnp.exp(part - top) for part in parts]
    total = jnp.sum(functools.reduce(jnp.add, weights), axis=1, keepdims=True)
    inverse = 1.0 / total
    weights = [w * inverse for w in weights]
    weights_low = jnp.concatenate([w.astype(jnp.bfloat16) for w in weights], axis=1)
    out2 = jnp.dot(weights_low, values, preferred_element_type=jnp.float32)
    attended = unstack_heads(out2, low).astype(jnp.bfloat16)
    out_ref[rows, out_cols] = attended
    product = grad.astype(jnp.float32) * attended.astype(jnp.float32)
    delta = jnp.sum(stack_heads(product, low), axis=1, keepdims=True)
    dprobs = dot_last(g2, values)
    dscores = jnp.concatenate(
        [
            (weights[t] * (dprobs[:, t * BLK : (t + 1) * BLK] - delta)).astype(jnp.bfloat16)
            for t in range(tiles)
        ],
        axis=1,
    )
    grad2 = jnp.dot(dscores, keys, preferred_element_type=jnp.float32)
    grad_q_ref[rows, out_cols] = (unstack_heads(grad2, low) * scale).astype(jnp.bfloat16)
    for which, product in ((0, dot_first(dscores, q2)), (1, dot_first(weights_low, g2))):
        local_ref[which, rows, near] = product[:BLK]
        for t in range(1, tiles):
            entry_ref[block, t - 1, which, :, near] = product[t * BLK : (t + 1) * BLK].astype(
                jnp.bfloat16
            )


def clear_entries(entry_ref, entries):
    for block in range(2):
        entry_ref[block, entries + 1] = jnp.zeros(entry_ref.shape[2:], jnp.bfloat16)


def assemble(axis_length, frames_ref, sink_ref, entry_ref, parts_ref):
    entries = frames_ref.shape[1]

    @pl.loop(0, axis_length)
    def _(j):
        picked = []
        for block in range(2):
            slot = entries + 1
            for e in reversed(range(entries)):
                slot = jnp.where(frames_ref[block, e] == j, e, slot)
            picked.append(jnp.where(sink_ref[0] == j, entries, slot))
        for which in range(2):
            parts_ref[j, which] = (
                entry_ref[0, picked[0], which].astype(jnp.float32)
                + entry_ref[1, picked[1], which].astype(jnp.float32)
            ).astype(jnp.bfloat16)


def gather_attend_kernel(
    axis_length,
    y_count,
    frames_ref,
    sink_ref,
    q_hbm,
    kv_hbm,
    g_hbm,
    out_ref,
    grad_q_ref,
    local_ref,
    parts_hbm,
    second_ref,
    first_ref,
    entry_ref,
    q_ref,
    kv_ref,
    g_ref,
    parts_ref,
    load_sem,
    own_sem,
    up_sem,
    down_sem,
    y_sem,
    core_sem,
    recv_sem,
):
    z_count = axis_length // (2 * y_count)
    me = lax.axis_index("seq")
    core = me % 2
    y = (me // 2) % y_count
    z = me // (2 * y_count)
    y_peer = (z * y_count + (y_count - 1 - y)) * 2 + core
    sibling = me + 1 - 2 * core
    offset = core * BLK
    width = first_ref.shape[3]
    items = 2 * width // PAIR
    step_items = -(-items // (z_count - 1))

    def index(z_at, y_at, core_at):
        return (z_at * y_count + y_at) * 2 + core_at

    barrier = pltpu.get_barrier_semaphore()

    for k in range(1, z_count):
        pl.semaphore_signal(
            barrier, inc=1, device_id={"seq": index((z + k) % z_count, y, core)}
        )
    peers = z_count
    pl.semaphore_signal(barrier, inc=1, device_id={"seq": sibling})
    if y_count > 1:
        pl.semaphore_signal(barrier, inc=1, device_id={"seq": y_peer})
        peers += 1
    pl.semaphore_wait(barrier, peers)

    def plan(half, buffer):
        def remote(piece, which, target, send_sem, own=False):
            place = buffer.at[piece, which]
            source = kv_hbm.at[which, pl.ds(offset, BLK), pl.ds(half * width, width)] if own else place
            return pltpu.make_async_remote_copy(
                src_ref=source,
                dst_ref=place,
                send_sem=send_sem,
                recv_sem=recv_sem.at[half, piece, which],
                device_id={"seq": target},
                device_id_type=pl.DeviceIdType.MESH,
            )

        def await_piece(piece, which):
            remote(piece, which, sibling, core_sem.at[half, 0, which]).wait_recv()

        def to_up(step, which, own=False):
            return remote(
                index(z - step, y, core), which, me + 2 * y_count, up_sem.at[half, step, which], own
            )

        def to_down(step, which, own=False):
            return remote(
                index(z + step, y, core), which, me - 2 * y_count, down_sem.at[half, step, which], own
            )

        def to_y(z_at, which, own=False):
            return remote(index(z_at, y, core), which, y_peer, y_sem.at[half, z_at, which], own)

        def to_core(z_at, y_at, which, own=False):
            return remote(
                index(z_at, y_at, core), which, sibling, core_sem.at[half, z_at * y_count + y_at, which], own
            )

        def own_copy(which):
            return pltpu.make_async_copy(
                kv_hbm.at[which, pl.ds(offset, BLK), pl.ds(half * width, width)], buffer.at[me, which], own_sem.at[half, which]
            )

        def begin():
            for which in range(2):
                pl.when(z < z_count - 1)(lambda: to_up(0, which, True).start())
                pl.when(z > 0)(lambda: to_down(0, which, True).start())
                if y_count > 1:
                    to_y(z, which, True).start()
                to_core(z, y, which, True).start()
            for which in range(2):
                own_copy(which).start()

        def pass_y(distance):
            if y_count == 1:
                return
            for which in range(2):
                def hand(z_at):
                    await_piece(index(z_at, 1 - y, core), which)
                    to_core(z_at, 1 - y, which).start()

                pl.when(z - distance >= 0)(lambda: hand(z - distance))
                if distance:
                    pl.when(z + distance < z_count)(lambda: hand(z + distance))

        def pass_step(step):
            for which in range(2):
                @pl.when(z - step >= 0)
                def _():
                    await_piece(index(z - step, y, core), which)
                    pl.when(z < z_count - 1)(lambda: to_up(step, which).start())
                    if y_count > 1:
                        to_y(z - step, which).start()
                    to_core(z - step, y, which).start()

                @pl.when(z + step < z_count)
                def _():
                    await_piece(index(z + step, y, core), which)
                    pl.when(z > 0)(lambda: to_down(step, which).start())
                    if y_count > 1:
                        to_y(z + step, which).start()
                    to_core(z + step, y, which).start()
            pass_y(step - 1)
        def arrive():
            for which in range(2):
                own_copy(which).wait()
                for z_at in range(z_count):
                    for y_at in range(y_count):
                        await_piece(index(z_at, y_at, 1 - core), which)
        def finish():
            for which in range(2):
                for z_at in range(z_count):
                    if y_count > 1:
                        to_y(z_at, which).wait_send()
                    for y_at in range(y_count):
                        to_core(z_at, y_at, which).wait_send()
                    pl.when((z - z_at >= 0) & (z < z_count - 1))(lambda: to_up(z_at, which).wait_send())
                    pl.when((z + z_at < z_count) & (z > 0))(lambda: to_down(z_at, which).wait_send())


        return begin, pass_step, pass_y, arrive, finish

    def work(low_item, high_item):
        @pl.loop(low_item, high_item)
        def _(item):
            attend_step(
                axis_length, 0, item, frames_ref, sink_ref, q_ref, kv_ref, g_ref, first_ref,
                (out_ref, grad_q_ref, local_ref, entry_ref),
            )

    begin, pass_step, pass_y, arrive, finish = plan(0, first_ref)
    begin_second, pass_step_second, pass_y_second, arrive_second, finish_second = plan(
        1, second_ref
    )
    loads = [
        pltpu.make_async_copy(source, place, load_sem.at[k])
        for k, (source, place) in enumerate(((q_hbm, q_ref), (kv_hbm, kv_ref), (g_hbm, g_ref)))
    ]
    begin()
    for load in loads:
        load.start()
    clear_entries(entry_ref, frames_ref.shape[1])
    for step in range(1, z_count):
        pass_step(step)
    begin_second()
    pass_y(z_count - 1)
    arrive()
    for load in loads:
        load.wait()
    done = 0
    for step in range(1, z_count):
        pass_step_second(step)
        upto = min(items, done + step_items)
        if upto > done:
            work(done, upto)
        done = upto
    pass_y_second(z_count - 1)
    assemble(axis_length, frames_ref, sink_ref, entry_ref, parts_ref)
    store = pltpu.make_async_copy(parts_ref, parts_hbm, load_sem.at[3])
    store.start()
    arrive_second()
    finish()
    finish_second()
    store.wait()


def gather_attend(axis_length, y_count, frames, sink, queries, keys_values, cotangent):
    z_count = axis_length // (2 * y_count)
    rows, width = queries.shape
    half = width // 2
    entries = frames.shape[1]
    vmem = pl.BlockSpec(memory_space=pltpu.VMEM)
    smem = pl.BlockSpec(memory_space=pltpu.SMEM)
    hbm = pl.BlockSpec(memory_space=pl.ANY)
    dma = pltpu.SemaphoreType.DMA
    gathered = (axis_length, 2, BLK, half)
    return pl.pallas_call(
        functools.partial(gather_attend_kernel, axis_length, y_count),
        out_shape=(
            jax.ShapeDtypeStruct((rows, half), jnp.bfloat16),
            jax.ShapeDtypeStruct((rows, half), jnp.bfloat16),
            jax.ShapeDtypeStruct((2, rows, half), jnp.float32),
            jax.ShapeDtypeStruct(gathered, jnp.bfloat16),
            jax.ShapeDtypeStruct(gathered, jnp.bfloat16),
        ),
        in_specs=[smem, smem, hbm, hbm, hbm],
        out_specs=[vmem, vmem, vmem, hbm, hbm],
        scratch_shapes=[
            pltpu.VMEM(gathered, jnp.bfloat16),
            pltpu.VMEM((2, entries + 2, 2, BLK, half), jnp.bfloat16),
            pltpu.VMEM(queries.shape, jnp.bfloat16),
            pltpu.VMEM(keys_values.shape, jnp.bfloat16),
            pltpu.VMEM(cotangent.shape, jnp.bfloat16),
            pltpu.VMEM(gathered, jnp.bfloat16),
            dma((4,)),
            dma((2, 2)),
            dma((2, z_count, 2)),
            dma((2, z_count, 2)),
            dma((2, z_count, 2)),
            dma((2, z_count * y_count, 2)),
            dma((2, axis_length, 2)),
        ],
        compiler_params=pltpu.CompilerParams(
            collective_id=0, has_side_effects=True, vmem_limit_bytes=VMEM_BYTES
        ),
        name="gather_attend",
    )(frames, sink, queries, keys_values, cotangent)


def attend_reduce_kernel(
    axis_length,
    y_count,
    frames_ref,
    sink_ref,
    q_hbm,
    kv_hbm,
    g_hbm,
    anchors_hbm,
    first_out_ref,
    first_grad_ref,
    first_local_hbm,
    first_parts_hbm,
    attended_ref,
    grad_q_ref,
    grad_kv_ref,
    second_local_ref,
    second_parts_ref,
    entry_ref,
    q_ref,
    kv_ref,
    g_ref,
    anchors_ref,
    first_local_ref,
    first_parts_ref,
    load_sem,
    from_core,
    from_y,
    from_z,
    core_sum,
    z_term,
    core_send,
    core_recv,
    y_send,
    y_recv,
    z_send,
    z_recv,
):
    z_count = axis_length // (2 * y_count)
    me = lax.axis_index("seq")
    core = me % 2
    y = (me // 2) % y_count
    z = me // (2 * y_count)
    other_y = y_count - 1 - y
    y_peer = (z * y_count + other_y) * 2 + core
    sibling = me + 1 - 2 * core
    offset = core * BLK
    rest = (1 - core) * BLK
    width = anchors_ref.shape[3]
    items = 2 * width // PAIR
    step_items = -(-items // (z_count - 1))
    stride = jnp.where(z < z_count // 2, -1, 1)
    order = [(z + stride * (1 + k) + z_count) % z_count for k in range(z_count)]

    pairs_of_refs = (
        (first_parts_hbm, first_parts_ref),
        (anchors_hbm, anchors_ref),
        (q_hbm, q_ref),
        (kv_hbm, kv_ref),
        (g_hbm, g_ref),
        (first_local_hbm, first_local_ref),
    )
    loads = [
        pltpu.make_async_copy(source, place, load_sem.at[k])
        for k, (source, place) in enumerate(pairs_of_refs)
    ]
    for load in loads:
        load.start()
    barrier = pltpu.get_barrier_semaphore()
    peers = z_count - 1 + y_count
    for k in range(z_count - 1):
        pl.semaphore_signal(
            barrier, inc=1, device_id={"seq": (order[k] * y_count + y) * 2 + core}
        )
    pl.semaphore_signal(barrier, inc=1, device_id={"seq": sibling})
    if y_count > 1:
        pl.semaphore_signal(barrier, inc=1, device_id={"seq": y_peer})
    pl.semaphore_wait(barrier, peers)

    def plan(half, local_ref, parts_ref, send_ref):
        def remote(source, place, send_sem, recv_sem, target):
            return pltpu.make_async_remote_copy(
                src_ref=source,
                dst_ref=place,
                send_sem=send_sem,
                recv_sem=recv_sem,
                device_id={"seq": target},
                device_id_type=pl.DeviceIdType.MESH,
            )

        def to_core(piece):
            return remote(
                send_ref.at[piece * 2 + 1 - core],
                from_core.at[half, piece],
                core_send.at[half, piece],
                core_recv.at[half, piece],
                sibling,
            )

        def to_y(k, which):
            return remote(
                core_sum.at[half, order[k] * y_count + other_y, which],
                from_y.at[half, order[k], which],
                y_send.at[half, k, which],
                y_recv.at[half, k, which],
                y_peer,
            )

        def to_z(k, which):
            return remote(
                z_term.at[half, order[k], which],
                from_z.at[half, z, which],
                z_send.at[half, k, which],
                z_recv.at[half, z, which],
                (order[k] * y_count + y) * 2 + core,
            )

        def from_z_wait(k, which):
            remote(
                z_term.at[half, order[k], which],
                from_z.at[half, order[k], which],
                z_send.at[half, k, which],
                z_recv.at[half, order[k], which],
                sibling,
            ).wait_recv()

        def wide(value):
            return value.astype(jnp.float32)

        def merge_core(piece):
            to_core(piece).wait_recv()
            for which in range(2):
                core_sum[half, piece, which] = (
                    wide(parts_ref[piece * 2 + core, which]) + wide(from_core[half, piece, which])
                ).astype(jnp.bfloat16)

        def begin():
            if y_count > 1:
                for k in range(z_count):
                    to_core(order[k] * y_count + other_y).start()
            for k in range(z_count):
                to_core(order[k] * y_count + y).start()

        def merge():
            if y_count > 1:
                for k in range(z_count):
                    merge_core(order[k] * y_count + other_y)
                    for which in range(2):
                        to_y(k, which).start()
            for k in range(z_count):
                merge_core(order[k] * y_count + y)

        def term_of(k, which):
            term = wide(core_sum[half, order[k] * y_count + y, which])
            if y_count > 1:
                to_y(k, which).wait_recv()
                term = term + wide(from_y[half, order[k], which])
            return term

        def pass_z(k):
            for which in range(2):
                z_term[half, order[k], which] = term_of(k, which).astype(jnp.bfloat16)
                to_z(k, which).start()

        def total():
            cols = pl.ds(half * width, width)
            for which in range(2):
                grad_kv_ref[which, pl.ds(rest, BLK), cols] = local_ref[
                    which, pl.ds(rest, BLK)
                ].astype(jnp.bfloat16)
                summed = term_of(z_count - 1, which) + local_ref[which, pl.ds(offset, BLK)]
                for other in range(z_count - 1):
                    from_z_wait(other, which)
                    summed = summed + wide(from_z[half, order[other], which])
                grad_kv_ref[which, pl.ds(offset, BLK), cols] = summed.astype(jnp.bfloat16)

        def finish():
            for k in range(z_count):
                for y_at in range(y_count):
                    to_core(order[k] * y_count + y_at).wait_send()
                for which in range(2):
                    if y_count > 1:
                        to_y(k, which).wait_send()
                    if k < z_count - 1:
                        to_z(k, which).wait_send()

        return begin, merge, pass_z, total, finish

    def work(low_item, high_item):
        @pl.loop(low_item, high_item)
        def _(item):
            attend_step(
                axis_length, 1, item, frames_ref, sink_ref, q_ref, kv_ref, g_ref, anchors_ref,
                (attended_ref, grad_q_ref, second_local_ref, entry_ref),
            )

    begin, merge, pass_z, total, finish = plan(
        0, first_local_ref, first_parts_ref, first_parts_hbm
    )
    begin_second, merge_second, pass_z_second, total_second, finish_second = plan(
        1, second_local_ref, second_parts_ref, second_parts_ref
    )
    begin()
    loads[0].wait()
    merge()
    clear_entries(entry_ref, frames_ref.shape[1])
    attended_ref[:, pl.ds(0, width)] = first_out_ref[...]
    grad_q_ref[:, pl.ds(0, width)] = first_grad_ref[...]
    for load in loads[1:]:
        load.wait()
    done = 0
    for k in range(z_count - 1):
        upto = min(items, done + step_items)
        if upto > done:
            work(done, upto)
        done = upto
        pass_z(k)
    assemble(axis_length, frames_ref, sink_ref, entry_ref, second_parts_ref)
    begin_second()
    merge_second()
    for k in range(z_count - 1):
        if k == z_count // 2:
            total()
        pass_z_second(k)
    total_second()
    finish()
    finish_second()


def attend_reduce(axis_length, y_count, frames, sink, queries, keys_values, cotangent, gathered):
    attended, grad_queries, local, parts, anchors = gathered
    z_count = axis_length // (2 * y_count)
    chips = axis_length // 2
    tile = parts.shape[1:]
    entries = frames.shape[1]
    vmem = pl.BlockSpec(memory_space=pltpu.VMEM)
    smem = pl.BlockSpec(memory_space=pltpu.SMEM)
    hbm = pl.BlockSpec(memory_space=pl.ANY)
    dma = pltpu.SemaphoreType.DMA
    return pl.pallas_call(
        functools.partial(attend_reduce_kernel, axis_length, y_count),
        out_shape=(
            jax.ShapeDtypeStruct(queries.shape, jnp.bfloat16),
            jax.ShapeDtypeStruct(queries.shape, jnp.bfloat16),
            jax.ShapeDtypeStruct(keys_values.shape, jnp.bfloat16),
        ),
        in_specs=[smem, smem] + [hbm] * 4 + [vmem] * 2 + [hbm] * 2,
        out_specs=[vmem] * 3,
        scratch_shapes=[
            pltpu.VMEM(local.shape, jnp.float32),
            pltpu.VMEM(parts.shape, jnp.bfloat16),
            pltpu.VMEM((2, entries + 2) + tile, jnp.bfloat16),
            pltpu.VMEM(queries.shape, jnp.bfloat16),
            pltpu.VMEM(keys_values.shape, jnp.bfloat16),
            pltpu.VMEM(cotangent.shape, jnp.bfloat16),
            pltpu.VMEM(anchors.shape, jnp.bfloat16),
            pltpu.VMEM(local.shape, jnp.float32),
            pltpu.VMEM(parts.shape, jnp.bfloat16),
            dma((6,)),
            pltpu.VMEM((2, chips) + tile, jnp.bfloat16),
            pltpu.VMEM((2, z_count if y_count > 1 else 1) + tile, jnp.bfloat16),
            pltpu.VMEM((2, z_count) + tile, jnp.bfloat16),
            pltpu.VMEM((2, chips) + tile, jnp.bfloat16),
            pltpu.VMEM((2, z_count) + tile, jnp.bfloat16),
            dma((2, chips)),
            dma((2, chips)),
            dma((2, z_count, 2)),
            dma((2, z_count, 2)),
            dma((2, z_count, 2)),
            dma((2, z_count, 2)),
        ],
        compiler_params=pltpu.CompilerParams(
            collective_id=1, has_side_effects=True, vmem_limit_bytes=VMEM_BYTES
        ),
        name="attend_reduce",
    )(
        frames, sink, queries, keys_values, cotangent, anchors,
        attended, grad_queries, local, parts,
    )


def publish_kernel(*refs):
    sources, places, sem = refs[:3], refs[3:6], refs[6]
    copies = []
    for source, place in zip(sources, places):
        rows = source.shape[0] // 4
        for part in range(4):
            here = pl.ds(part * rows, rows)
            copies.append(
                pltpu.make_async_copy(source.at[here], place.at[here], sem.at[len(copies)])
            )
    for copy in copies:
        copy.start()
    for copy in copies:
        copy.wait()


def publish(attended, grad_queries, grad_keys_values):
    hbm = pl.BlockSpec(memory_space=pl.ANY)
    shape = grad_keys_values.shape
    flat = grad_keys_values.reshape(shape[0] * shape[1], shape[2])
    arrays = (attended, grad_queries, flat)
    outs = pl.pallas_call(
        publish_kernel,
        out_shape=tuple(jax.ShapeDtypeStruct(a.shape, a.dtype) for a in arrays),
        in_specs=[hbm] * 3,
        out_specs=[hbm] * 3,
        scratch_shapes=[pltpu.SemaphoreType.DMA((12,))],
        name="publish",
    )(*arrays)
    return outs[0], outs[1], outs[2].reshape(shape)


def shards(y_count, queries, keys_values, cotangent, frame_lists, sink_owner):
    axis_length = lax.axis_size("seq")
    args = (axis_length, y_count, frame_lists, sink_owner, queries, keys_values, cotangent)
    return publish(*attend_reduce(*args, gather_attend(*args)))


def solution(mesh):
    rows = P(("groups", "seq"), None)
    pairs = P(None, ("groups", "seq"), None)
    y_count = 2 if mesh.shape["groups"] == 2 and mesh.shape["seq"] % 4 == 0 else 1
    return jax.shard_map(
        functools.partial(shards, y_count),
        mesh=mesh,
        in_specs=(rows, pairs, rows, rows, P("groups")),
        out_specs=(rows, rows, pairs),
        check_vma=False,
    )
```

```python
import functools
import math

import jax
import jax.numpy as jnp
from jax import lax
from jax.experimental import pallas as pl
from jax.experimental.pallas import tpu as pltpu
from jax.sharding import PartitionSpec as P

HEAD = 64
BLK = 128
PAIR = 2 * HEAD
NEG = -1e30
VMEM_BYTES = 60 * 1024 * 1024


def anchor_span(device_id, axis_length):
    return jnp.where(device_id % 2 == 0, device_id, 2 * axis_length - 1 - device_id)


def stack_heads(rows, low):
    zero = jnp.zeros_like(rows)
    return jnp.concatenate((jnp.where(low, rows, zero), jnp.where(low, zero, rows)), axis=0)


def unstack_heads(rows, low):
    return jnp.where(low, rows[:BLK], rows[BLK:])


def dot_last(left, right):
    return lax.dot_general(left, right, (((1,), (1,)), ((), ())), preferred_element_type=jnp.float32)


def dot_first(left, right):
    return lax.dot_general(left, right, (((0,), (0,)), ((), ())), preferred_element_type=jnp.float32)


def attend_step(
    axis_length, half, item, frames_ref, sink_ref, q_ref, kv_ref, g_ref, anchors_ref, outs
):
    out_ref, grad_q_ref, local_ref, entry_ref = outs
    me = lax.axis_index("seq")
    sink = sink_ref[0]
    entries = frames_ref.shape[1]
    pairs = anchors_ref.shape[3] // PAIR
    scale = 1.0 / math.sqrt(HEAD)
    low = lax.broadcasted_iota(jnp.int32, (BLK, PAIR), 1) < HEAD
    row = lax.broadcasted_iota(jnp.int32, (2 * BLK, BLK), 0) % BLK
    causal = lax.broadcasted_iota(jnp.int32, (2 * BLK, BLK), 1) <= row
    block = jnp.where(item >= pairs, 1, 0)
    pair = item - block * pairs
    span = jnp.where(block == 0, me, 2 * axis_length - 1 - me)
    rows = pl.ds(pl.multiple_of(block * BLK, BLK), BLK)
    ids = [frames_ref[block, e] for e in range(entries)]
    biases = []
    for e in range(entries):
        valid = (anchor_span(ids[e], axis_length) < span) & (ids[e] != sink)
        for earlier in range(e):
            valid = valid & (ids[e] != ids[earlier])
        biases.append(jnp.where(valid, 0.0, NEG))
    slots = ids + [sink]
    window_scalar = jnp.where(span == anchor_span(sink, axis_length), NEG, 0.0)
    window_bias = jnp.where(causal, window_scalar, NEG)
    cols = pl.ds(pl.multiple_of((half * pairs + pair) * PAIR, PAIR), PAIR)
    near = pl.ds(pl.multiple_of(pair * PAIR, PAIR), PAIR)
    out_cols = cols if out_ref.shape[1] == q_ref.shape[1] else near
    q2 = stack_heads(q_ref[rows, cols] * jnp.bfloat16(scale), low)
    grad = g_ref[rows, cols]
    g2 = stack_heads(grad, low)
    keys = jnp.concatenate(
        [kv_ref[0, rows, cols]] + [anchors_ref[j, 0, :, near] for j in slots], axis=0
    )
    values = jnp.concatenate(
        [kv_ref[1, rows, cols]] + [anchors_ref[j, 1, :, near] for j in slots], axis=0
    )
    tiles = 1 + len(slots)
    scores = dot_last(q2, keys)
    parts = [scores[:, t * BLK : (t + 1) * BLK] for t in range(tiles)]
    parts[0] = parts[0] + window_bias
    for t in range(1, tiles - 1):
        parts[t] = parts[t] + biases[t - 1]
    top = functools.reduce(jnp.maximum, parts)
    top = jnp.max(top, axis=1, keepdims=True)
    weights = [jnp.exp(part - top) for part in parts]
    total = jnp.sum(functools.reduce(jnp.add, weights), axis=1, keepdims=True)
    inverse = 1.0 / total
    weights = [w * inverse for w in weights]
    weights_low = jnp.concatenate([w.astype(jnp.bfloat16) for w in weights], axis=1)
    out2 = jnp.dot(weights_low, values, preferred_element_type=jnp.float32)
    attended = unstack_heads(out2, low).astype(jnp.bfloat16)
    out_ref[rows, out_cols] = attended
    product = grad.astype(jnp.float32) * attended.astype(jnp.float32)
    delta = jnp.sum(stack_heads(product, low), axis=1, keepdims=True)
    dprobs = dot_last(g2, values)
    dscores = jnp.concatenate(
        [
            (weights[t] * (dprobs[:, t * BLK : (t + 1) * BLK] - delta)).astype(jnp.bfloat16)
            for t in range(tiles)
        ],
        axis=1,
    )
    grad2 = jnp.dot(dscores, keys, preferred_element_type=jnp.float32)
    grad_q_ref[rows, out_cols] = (unstack_heads(grad2, low) * scale).astype(jnp.bfloat16)
    for which, product in ((0, dot_first(dscores, q2)), (1, dot_first(weights_low, g2))):
        local_ref[which, rows, near] = product[:BLK]
        for t in range(1, tiles):
            entry_ref[block, t - 1, which, :, near] = product[t * BLK : (t + 1) * BLK].astype(
                jnp.bfloat16
            )


def clear_entries(entry_ref, entries):
    for block in range(2):
        entry_ref[block, entries + 1] = jnp.zeros(entry_ref.shape[2:], jnp.bfloat16)


def assemble(axis_length, frames_ref, sink_ref, entry_ref, parts_ref):
    entries = frames_ref.shape[1]

    @pl.loop(0, axis_length)
    def _(j):
        picked = []
        for block in range(2):
            slot = entries + 1
            for e in reversed(range(entries)):
                slot = jnp.where(frames_ref[block, e] == j, e, slot)
            picked.append(jnp.where(sink_ref[0] == j, entries, slot))
        for which in range(2):
            parts_ref[j, which] = (
                entry_ref[0, picked[0], which].astype(jnp.float32)
                + entry_ref[1, picked[1], which].astype(jnp.float32)
            ).astype(jnp.bfloat16)


def gather_attend_kernel(
    axis_length,
    y_count,
    frames_ref,
    sink_ref,
    q_hbm,
    kv_hbm,
    g_hbm,
    out_ref,
    grad_q_ref,
    local_ref,
    parts_hbm,
    second_ref,
    first_ref,
    entry_ref,
    q_ref,
    kv_ref,
    g_ref,
    parts_ref,
    load_sem,
    own_sem,
    up_sem,
    down_sem,
    y_sem,
    core_sem,
    recv_sem,
):
    z_count = axis_length // (2 * y_count)
    me = lax.axis_index("seq")
    core = me % 2
    y = (me // 2) % y_count
    z = me // (2 * y_count)
    y_peer = (z * y_count + (y_count - 1 - y)) * 2 + core
    sibling = me + 1 - 2 * core
    offset = core * BLK
    width = first_ref.shape[3]
    items = 2 * width // PAIR
    step_items = -(-items // (z_count - 1))

    def index(z_at, y_at, core_at):
        return (z_at * y_count + y_at) * 2 + core_at

    barrier = pltpu.get_barrier_semaphore()

    for k in range(1, z_count):
        pl.semaphore_signal(
            barrier, inc=1, device_id={"seq": index((z + k) % z_count, y, core)}
        )
    peers = z_count
    pl.semaphore_signal(barrier, inc=1, device_id={"seq": sibling})
    if y_count > 1:
        pl.semaphore_signal(barrier, inc=1, device_id={"seq": y_peer})
        peers += 1
    pl.semaphore_wait(barrier, peers)

    def plan(half, buffer):
        def remote(piece, which, target, send_sem, own=False):
            place = buffer.at[piece, which]
            source = kv_hbm.at[which, pl.ds(offset, BLK), pl.ds(half * width, width)] if own else place
            return pltpu.make_async_remote_copy(
                src_ref=source,
                dst_ref=place,
                send_sem=send_sem,
                recv_sem=recv_sem.at[half, piece, which],
                device_id={"seq": target},
                device_id_type=pl.DeviceIdType.MESH,
            )

        def await_piece(piece, which):
            remote(piece, which, sibling, core_sem.at[half, 0, which]).wait_recv()

        def to_up(step, which, own=False):
            return remote(
                index(z - step, y, core), which, me + 2 * y_count, up_sem.at[half, step, which], own
            )

        def to_down(step, which, own=False):
            return remote(
                index(z + step, y, core), which, me - 2 * y_count, down_sem.at[half, step, which], own
            )

        def to_y(z_at, which, own=False):
            return remote(index(z_at, y, core), which, y_peer, y_sem.at[half, z_at, which], own)

        def to_core(z_at, y_at, which, own=False):
            return remote(
                index(z_at, y_at, core), which, sibling, core_sem.at[half, z_at * y_count + y_at, which], own
            )

        def own_copy(which):
            return pltpu.make_async_copy(
                kv_hbm.at[which, pl.ds(offset, BLK), pl.ds(half * width, width)], buffer.at[me, which], own_sem.at[half, which]
            )

        def begin():
            for which in range(2):
                pl.when(z < z_count - 1)(lambda: to_up(0, which, True).start())
                pl.when(z > 0)(lambda: to_down(0, which, True).start())
                if y_count > 1:
                    to_y(z, which, True).start()
                to_core(z, y, which, True).start()
            for which in range(2):
                own_copy(which).start()

        def pass_y(distance):
            if y_count == 1:
                return
            for which in range(2):
                def hand(z_at):
                    await_piece(index(z_at, 1 - y, core), which)
                    to_core(z_at, 1 - y, which).start()

                pl.when(z - distance >= 0)(lambda: hand(z - distance))
                if distance:
                    pl.when(z + distance < z_count)(lambda: hand(z + distance))

        def pass_step(step):
            for which in range(2):
                @pl.when(z - step >= 0)
                def _():
                    await_piece(index(z - step, y, core), which)
                    pl.when(z < z_count - 1)(lambda: to_up(step, which).start())
                    if y_count > 1:
                        to_y(z - step, which).start()
                    to_core(z - step, y, which).start()

                @pl.when(z + step < z_count)
                def _():
                    await_piece(index(z + step, y, core), which)
                    pl.when(z > 0)(lambda: to_down(step, which).start())
                    if y_count > 1:
                        to_y(z + step, which).start()
                    to_core(z + step, y, which).start()
            pass_y(step - 1)
        def arrive():
            for which in range(2):
                own_copy(which).wait()
                for z_at in range(z_count):
                    for y_at in range(y_count):
                        await_piece(index(z_at, y_at, 1 - core), which)
        def finish():
            for which in range(2):
                for z_at in range(z_count):
                    if y_count > 1:
                        to_y(z_at, which).wait_send()
                    for y_at in range(y_count):
                        to_core(z_at, y_at, which).wait_send()
                    pl.when((z - z_at >= 0) & (z < z_count - 1))(lambda: to_up(z_at, which).wait_send())
                    pl.when((z + z_at < z_count) & (z > 0))(lambda: to_down(z_at, which).wait_send())


        return begin, pass_step, pass_y, arrive, finish

    def work(low_item, high_item):
        @pl.loop(low_item, high_item)
        def _(item):
            attend_step(
                axis_length, 0, item, frames_ref, sink_ref, q_ref, kv_ref, g_ref, first_ref,
                (out_ref, grad_q_ref, local_ref, entry_ref),
            )

    begin, pass_step, pass_y, arrive, finish = plan(0, first_ref)
    begin_second, pass_step_second, pass_y_second, arrive_second, finish_second = plan(
        1, second_ref
    )
    loads = [
        pltpu.make_async_copy(source, place, load_sem.at[k])
        for k, (source, place) in enumerate(((q_hbm, q_ref), (kv_hbm, kv_ref), (g_hbm, g_ref)))
    ]
    begin()
    for load in loads:
        load.start()
    clear_entries(entry_ref, frames_ref.shape[1])
    for step in range(1, z_count):
        pass_step(step)
    begin_second()
    pass_y(z_count - 1)
    arrive()
    for load in loads:
        load.wait()
    done = 0
    for step in range(1, z_count):
        pass_step_second(step)
        upto = min(items, done + step_items)
        if upto > done:
            work(done, upto)
        done = upto
    pass_y_second(z_count - 1)
    assemble(axis_length, frames_ref, sink_ref, entry_ref, parts_ref)
    store = pltpu.make_async_copy(parts_ref, parts_hbm, load_sem.at[3])
    store.start()
    arrive_second()
    finish()
    finish_second()
    store.wait()


def gather_attend(axis_length, y_count, frames, sink, queries, keys_values, cotangent):
    z_count = axis_length // (2 * y_count)
    rows, width = queries.shape
    half = width // 2
    entries = frames.shape[1]
    vmem = pl.BlockSpec(memory_space=pltpu.VMEM)
    smem = pl.BlockSpec(memory_space=pltpu.SMEM)
    hbm = pl.BlockSpec(memory_space=pl.ANY)
    dma = pltpu.SemaphoreType.DMA
    gathered = (axis_length, 2, BLK, half)
    return pl.pallas_call(
        functools.partial(gather_attend_kernel, axis_length, y_count),
        out_shape=(
            jax.ShapeDtypeStruct((rows, half), jnp.bfloat16),
            jax.ShapeDtypeStruct((rows, half), jnp.bfloat16),
            jax.ShapeDtypeStruct((2, rows, half), jnp.float32),
            jax.ShapeDtypeStruct(gathered, jnp.bfloat16),
            jax.ShapeDtypeStruct(gathered, jnp.bfloat16),
        ),
        in_specs=[smem, smem, hbm, hbm, hbm],
        out_specs=[vmem, vmem, vmem, hbm, hbm],
        scratch_shapes=[
            pltpu.VMEM(gathered, jnp.bfloat16),
            pltpu.VMEM((2, entries + 2, 2, BLK, half), jnp.bfloat16),
            pltpu.VMEM(queries.shape, jnp.bfloat16),
            pltpu.VMEM(keys_values.shape, jnp.bfloat16),
            pltpu.VMEM(cotangent.shape, jnp.bfloat16),
            pltpu.VMEM(gathered, jnp.bfloat16),
            dma((4,)),
            dma((2, 2)),
            dma((2, z_count, 2)),
            dma((2, z_count, 2)),
            dma((2, z_count, 2)),
            dma((2, z_count * y_count, 2)),
            dma((2, axis_length, 2)),
        ],
        compiler_params=pltpu.CompilerParams(
            collective_id=0, has_side_effects=True, vmem_limit_bytes=VMEM_BYTES
        ),
        name="gather_attend",
    )(frames, sink, queries, keys_values, cotangent)


def attend_reduce_kernel(
    axis_length,
    y_count,
    frames_ref,
    sink_ref,
    q_hbm,
    kv_hbm,
    g_hbm,
    anchors_hbm,
    first_out_ref,
    first_grad_ref,
    first_local_hbm,
    first_parts_hbm,
    attended_ref,
    grad_q_ref,
    grad_kv_ref,
    second_local_ref,
    second_parts_ref,
    entry_ref,
    q_ref,
    kv_ref,
    g_ref,
    anchors_ref,
    first_local_ref,
    first_parts_ref,
    load_sem,
    from_core,
    from_y,
    from_z,
    core_sum,
    z_term,
    core_send,
    core_recv,
    y_send,
    y_recv,
    z_send,
    z_recv,
):
    z_count = axis_length // (2 * y_count)
    me = lax.axis_index("seq")
    core = me % 2
    y = (me // 2) % y_count
    z = me // (2 * y_count)
    other_y = y_count - 1 - y
    y_peer = (z * y_count + other_y) * 2 + core
    sibling = me + 1 - 2 * core
    offset = core * BLK
    rest = (1 - core) * BLK
    width = anchors_ref.shape[3]
    items = 2 * width // PAIR
    step_items = -(-items // (z_count - 1))
    stride = jnp.where(z < z_count // 2, -1, 1)
    order = [(z + stride * (1 + k) + z_count) % z_count for k in range(z_count)]

    pairs_of_refs = (
        (first_parts_hbm, first_parts_ref),
        (anchors_hbm, anchors_ref),
        (q_hbm, q_ref),
        (kv_hbm, kv_ref),
        (g_hbm, g_ref),
        (first_local_hbm, first_local_ref),
    )
    loads = [
        pltpu.make_async_copy(source, place, load_sem.at[k])
        for k, (source, place) in enumerate(pairs_of_refs)
    ]
    for load in loads:
        load.start()
    barrier = pltpu.get_barrier_semaphore()
    peers = z_count - 1 + y_count
    for k in range(z_count - 1):
        pl.semaphore_signal(
            barrier, inc=1, device_id={"seq": (order[k] * y_count + y) * 2 + core}
        )
    pl.semaphore_signal(barrier, inc=1, device_id={"seq": sibling})
    if y_count > 1:
        pl.semaphore_signal(barrier, inc=1, device_id={"seq": y_peer})
    pl.semaphore_wait(barrier, peers)

    def plan(half, local_ref, parts_ref, send_ref):
        def remote(source, place, send_sem, recv_sem, target):
            return pltpu.make_async_remote_copy(
                src_ref=source,
                dst_ref=place,
                send_sem=send_sem,
                recv_sem=recv_sem,
                device_id={"seq": target},
                device_id_type=pl.DeviceIdType.MESH,
            )

        def to_core(piece):
            return remote(
                send_ref.at[piece * 2 + 1 - core],
                from_core.at[half, piece],
                core_send.at[half, piece],
                core_recv.at[half, piece],
                sibling,
            )

        def to_y(k, which):
            return remote(
                core_sum.at[half, order[k] * y_count + other_y, which],
                from_y.at[half, order[k], which],
                y_send.at[half, k, which],
                y_recv.at[half, k, which],
                y_peer,
            )

        def to_z(k, which):
            return remote(
                z_term.at[half, order[k], which],
                from_z.at[half, z, which],
                z_send.at[half, k, which],
                z_recv.at[half, z, which],
                (order[k] * y_count + y) * 2 + core,
            )

        def from_z_wait(k, which):
            remote(
                z_term.at[half, order[k], which],
                from_z.at[half, order[k], which],
                z_send.at[half, k, which],
                z_recv.at[half, order[k], which],
                sibling,
            ).wait_recv()

        def wide(value):
            return value.astype(jnp.float32)

        def merge_core(piece):
            to_core(piece).wait_recv()
            for which in range(2):
                core_sum[half, piece, which] = (
                    wide(parts_ref[piece * 2 + core, which]) + wide(from_core[half, piece, which])
                ).astype(jnp.bfloat16)

        def begin():
            if y_count > 1:
                for k in range(z_count):
                    to_core(order[k] * y_count + other_y).start()
            for k in range(z_count):
                to_core(order[k] * y_count + y).start()

        def merge():
            if y_count > 1:
                for k in range(z_count):
                    merge_core(order[k] * y_count + other_y)
                    for which in range(2):
                        to_y(k, which).start()
            for k in range(z_count):
                merge_core(order[k] * y_count + y)

        def term_of(k, which):
            term = wide(core_sum[half, order[k] * y_count + y, which])
            if y_count > 1:
                to_y(k, which).wait_recv()
                term = term + wide(from_y[half, order[k], which])
            return term

        def pass_z(k):
            for which in range(2):
                z_term[half, order[k], which] = term_of(k, which).astype(jnp.bfloat16)
                to_z(k, which).start()

        def total():
            cols = pl.ds(half * width, width)
            for which in range(2):
                grad_kv_ref[which, pl.ds(rest, BLK), cols] = local_ref[
                    which, pl.ds(rest, BLK)
                ].astype(jnp.bfloat16)
                summed = term_of(z_count - 1, which) + local_ref[which, pl.ds(offset, BLK)]
                for other in range(z_count - 1):
                    from_z_wait(other, which)
                    summed = summed + wide(from_z[half, order[other], which])
                grad_kv_ref[which, pl.ds(offset, BLK), cols] = summed.astype(jnp.bfloat16)

        def finish():
            for k in range(z_count):
                for y_at in range(y_count):
                    to_core(order[k] * y_count + y_at).wait_send()
                for which in range(2):
                    if y_count > 1:
                        to_y(k, which).wait_send()
                    if k < z_count - 1:
                        to_z(k, which).wait_send()

        return begin, merge, pass_z, total, finish

    def work(low_item, high_item):
        @pl.loop(low_item, high_item)
        def _(item):
            attend_step(
                axis_length, 1, item, frames_ref, sink_ref, q_ref, kv_ref, g_ref, anchors_ref,
                (attended_ref, grad_q_ref, second_local_ref, entry_ref),
            )

    begin, merge, pass_z, total, finish = plan(
        0, first_local_ref, first_parts_ref, first_parts_hbm
    )
    begin_second, merge_second, pass_z_second, total_second, finish_second = plan(
        1, second_local_ref, second_parts_ref, second_parts_ref
    )
    begin()
    loads[0].wait()
    merge()
    clear_entries(entry_ref, frames_ref.shape[1])
    attended_ref[:, pl.ds(0, width)] = first_out_ref[...]
    grad_q_ref[:, pl.ds(0, width)] = first_grad_ref[...]
    for load in loads[1:]:
        load.wait()
    done = 0
    for k in range(z_count - 1):
        upto = min(items, done + step_items)
        if upto > done:
            work(done, upto)
        done = upto
        pass_z(k)
    assemble(axis_length, frames_ref, sink_ref, entry_ref, second_parts_ref)
    begin_second()
    merge_second()
    for k in range(z_count - 1):
        if k == z_count // 2:
            total()
        pass_z_second(k)
    total_second()
    finish()
    finish_second()


def attend_reduce(axis_length, y_count, frames, sink, queries, keys_values, cotangent, gathered):
    attended, grad_queries, local, parts, anchors = gathered
    z_count = axis_length // (2 * y_count)
    chips = axis_length // 2
    tile = parts.shape[1:]
    entries = frames.shape[1]
    vmem = pl.BlockSpec(memory_space=pltpu.VMEM)
    smem = pl.BlockSpec(memory_space=pltpu.SMEM)
    hbm = pl.BlockSpec(memory_space=pl.ANY)
    dma = pltpu.SemaphoreType.DMA
    return pl.pallas_call(
        functools.partial(attend_reduce_kernel, axis_length, y_count),
        out_shape=(
            jax.ShapeDtypeStruct(queries.shape, jnp.bfloat16),
            jax.ShapeDtypeStruct(queries.shape, jnp.bfloat16),
            jax.ShapeDtypeStruct(keys_values.shape, jnp.bfloat16),
        ),
        in_specs=[smem, smem] + [hbm] * 4 + [vmem] * 2 + [hbm] * 2,
        out_specs=[vmem] * 3,
        scratch_shapes=[
            pltpu.VMEM(local.shape, jnp.float32),
            pltpu.VMEM(parts.shape, jnp.bfloat16),
            pltpu.VMEM((2, entries + 2) + tile, jnp.bfloat16),
            pltpu.VMEM(queries.shape, jnp.bfloat16),
            pltpu.VMEM(keys_values.shape, jnp.bfloat16),
            pltpu.VMEM(cotangent.shape, jnp.bfloat16),
            pltpu.VMEM(anchors.shape, jnp.bfloat16),
            pltpu.VMEM(local.shape, jnp.float32),
            pltpu.VMEM(parts.shape, jnp.bfloat16),
            dma((6,)),
            pltpu.VMEM((2, chips) + tile, jnp.bfloat16),
            pltpu.VMEM((2, z_count if y_count > 1 else 1) + tile, jnp.bfloat16),
            pltpu.VMEM((2, z_count) + tile, jnp.bfloat16),
            pltpu.VMEM((2, chips) + tile, jnp.bfloat16),
            pltpu.VMEM((2, z_count) + tile, jnp.bfloat16),
            dma((2, chips)),
            dma((2, chips)),
            dma((2, z_count, 2)),
            dma((2, z_count, 2)),
            dma((2, z_count, 2)),
            dma((2, z_count, 2)),
        ],
        compiler_params=pltpu.CompilerParams(
            collective_id=1, has_side_effects=True, vmem_limit_bytes=VMEM_BYTES
        ),
        name="attend_reduce",
    )(
        frames, sink, queries, keys_values, cotangent, anchors,
        attended, grad_queries, local, parts,
    )


def publish_kernel(*refs):
    sources, places, holds, load_sem, store_sem = refs[:3], refs[3:6], refs[6:9], refs[9], refs[10]
    loads, stores = [], []
    for source, place, hold in zip(sources, places, holds):
        rows = source.shape[0] // 4
        for part in range(4):
            here = pl.ds(part * rows, rows)
            k = len(loads)
            loads.append(
                pltpu.make_async_copy(source.at[here], hold.at[here], load_sem.at[k])
            )
            stores.append(
                pltpu.make_async_copy(hold.at[here], place.at[here], store_sem.at[k])
            )
    for load in loads:
        load.start()
    for load, store in zip(loads, stores):
        load.wait()
        store.start()
    for store in stores:
        store.wait()


def publish(attended, grad_queries, grad_keys_values):
    hbm = pl.BlockSpec(memory_space=pl.ANY)
    shape = grad_keys_values.shape
    flat = grad_keys_values.reshape(shape[0] * shape[1], shape[2])
    arrays = (attended, grad_queries, flat)
    outs = pl.pallas_call(
        publish_kernel,
        out_shape=tuple(jax.ShapeDtypeStruct(a.shape, a.dtype) for a in arrays),
        in_specs=[hbm] * 3,
        out_specs=[hbm] * 3,
        scratch_shapes=[pltpu.VMEM(a.shape, a.dtype) for a in arrays]
        + [pltpu.SemaphoreType.DMA((12,)), pltpu.SemaphoreType.DMA((12,))],
        name="publish",
    )(*arrays)
    return outs[0], outs[1], outs[2].reshape(shape)


def shards(y_count, queries, keys_values, cotangent, frame_lists, sink_owner):
    axis_length = lax.axis_size("seq")
    args = (axis_length, y_count, frame_lists, sink_owner, queries, keys_values, cotangent)
    return publish(*attend_reduce(*args, gather_attend(*args)))


def solution(mesh):
    rows = P(("groups", "seq"), None)
    pairs = P(None, ("groups", "seq"), None)
    y_count = 2 if mesh.shape["groups"] == 2 and mesh.shape["seq"] % 4 == 0 else 1
    return jax.shard_map(
        functools.partial(shards, y_count),
        mesh=mesh,
        in_specs=(rows, pairs, rows, rows, P("groups")),
        out_specs=(rows, rows, pairs),
        check_vma=False,
    )
```
